32 devices in a mesh: rep: 8 (over z, y), zero: 4 (over x, core).
Axes of the slice: x: 2, y: 2, z: 4, core: 2. Of those that a mesh axis runs over, the one named last changes fastest.
Arguments:
- tokens: bfloat16 [12288, 1280], P(('rep', 'zero')), may hold values from -6 to 6
- cotangent: bfloat16 [12288, 1280], P(('rep', 'zero')), may hold values from -6 to 6
- weights: bfloat16 [1280, 6, 1280], P('zero')
- vectors: bfloat16 [5, 1280], P(None, 'zero')
- error: float32 [10240, 6, 1280], P(('rep', 'zero'))
- previous_right_factors: float32 [6, 1280, 32], P(None, None, 'zero'), may hold values from -6 to 6
- momentum: float32 [1280, 6, 1280], P('zero', None, 'rep')
- vec_momentum: float32 [5, 1280], P(None, 'zero')
- prompt_len: int32 [8], P('rep'), may hold values from 512 to 1024, as said below
Outputs:
- result: bfloat16 [12288, 1280], P(('rep', 'zero'))
- grad_tokens: float32 [12288, 1280], P(('rep', 'zero'))
- grad_weights: float32 [1280, 6, 1280], P('zero', None, 'rep')
- grad_vectors: float32 [5, 1280], P(None, 'zero')
- new_error: float32 [10240, 6, 1280], P(('rep', 'zero'))
- fresh_right_factors: float32 [6, 1280, 32], P(None, None, 'zero')
- new_momentum: float32 [1280, 6, 1280], P('zero', None, 'rep')
- new_vec_momentum: float32 [5, 1280], P(None, 'zero')
- update_weights: float32 [1280, 6, 1280], P('zero', None, 'rep')
- update_vectors: float32 [5, 1280], P(None, 'zero')
The draws below stay inside these ranges and needn't reach their ends.
Inputs may be any that keep to these rules, and one draw needn't show every extreme that they name: `prompt_len`: valid prompt rows of a group; the other prompt rows of its 1024 are padding.
All inputs are finite; a program needn't handle non-finite values.
Results may differ from the reference program's by a relative error of at most 0.028.
Values may be sent and summed in bfloat16 or wider, within the bound.
No kernel may reach another device: no remote copies, remote signals or barrier semaphores. Data moves between devices by JAX's collectives and lax.ppermute only.
A program may use at most 320 MiB of HBM per device.

```python
import math
import jax
import jax.numpy as jnp
from jax import lax

D = 1280
HEADS = 16
HEAD_DIM = 80
MATS = 6
VECS = 5
RANK = 8
PROMPT = 1024
CONT_LEN = 128
GROUPS = 8
PROMPT_DEV = 256
TOK_DEV = 384
TOKENS = 12288
N_REP = 8
N_ZERO = 4


def spread_draw(key, shape, scale):
    base = jax.random.truncated_normal(key, -3.0, 3.0, shape, jnp.float32)
    return base * scale


def draw_weights(key, part):
    factors = jnp.array([1.0, 1.0, 1.0, 8.0, 1.0, 1.5], jnp.float32)
    base = spread_draw(key, (D, MATS, D), 1.0)
    return (base * factors[None, :, None] / math.sqrt(D)).astype(jnp.bfloat16)


def draw_vectors(key, part):
    key_gain = jax.random.fold_in(key, 11)
    key_bias = jax.random.fold_in(key, 12)
    key_scale = jax.random.fold_in(key, 13)
    gains = jax.random.uniform(key_gain, (2, D), jnp.float32, 0.5, 1.5)
    biases = 0.5 * jax.random.truncated_normal(key_bias, -3.0, 3.0, (2, D), jnp.float32)
    scales = jax.random.uniform(key_scale, (1, D), jnp.float32, 0.0, 2.0)
    return jnp.concatenate([gains, biases, scales], axis=0).astype(jnp.bfloat16)


def draw_error(key, part):
    return spread_draw(key, (GROUPS * D, MATS, D), 0.3 * math.sqrt(PROMPT + PROMPT // PROMPT_DEV * CONT_LEN))


def draw_momentum(key, part):
    return spread_draw(key, (D, MATS, D), 0.1 * math.sqrt(PROMPT + PROMPT // PROMPT_DEV * CONT_LEN))


def draw_vec_momentum(key, part):
    return spread_draw(key, (VECS, D), 0.1 * math.sqrt(PROMPT + PROMPT // PROMPT_DEV * CONT_LEN))


def draw_prompt_len(key, part):
    key_len = jax.random.fold_in(key, 21)
    key_pick = jax.random.fold_in(key, 22)
    lengths = jax.random.randint(key_len, (GROUPS,), PROMPT // 2, PROMPT + 1, jnp.int32)
    order = jax.random.permutation(key_pick, GROUPS)
    lengths = lengths.at[order[0]].set(PROMPT)
    lengths = lengths.at[order[1]].set(PROMPT // 2)
    return lengths.astype(jnp.int32)


def steps_of(own_key, dims, split, smallest, top_value):
    def one(axis_at, blocks):
        draws = jax.random.uniform(jax.random.fold_in(jax.random.fold_in(own_key, 6), axis_at), (blocks,), jnp.float32, smallest / len(split), top_value / len(split))
        return jnp.repeat(jnp.exp(draws), dims[axis_at] // blocks).reshape((-1,) + (1,) * (len(dims) - axis_at - 1))

    loudness = one(*split[0])
    for cut in split[1:]:
        loudness = loudness * one(*cut)
    return loudness


def scatter_about(key, dims, spread, limit, pieces=(), kind=jnp.bfloat16):
    level = steps_of(key, dims, pieces, -0.22, 0.18) if pieces else 1.0
    values = jax.random.normal(key, dims, jnp.float32) * spread * level
    return jnp.minimum(jnp.maximum(values, -limit), limit).astype(kind)


def setup_inputs(seed: int = 0) -> dict:
    streams_of = jax.random.split(jax.random.key(seed), 10)
    return {
        "tokens": scatter_about(streams_of[0], (TOKENS, D), 1.0, 6.0, ((0, 32),)),
        "cotangent": scatter_about(streams_of[1], (TOKENS, D), 1.0, 6.0, ((0, 32),)),
        "weights": draw_weights(jax.random.fold_in(streams_of[9], 71), 0),
        "vectors": draw_vectors(jax.random.fold_in(streams_of[9], 71), 0),
        "error": draw_error(jax.random.fold_in(streams_of[9], 71), 0),
        "previous_right_factors": scatter_about(streams_of[5], (MATS, D, N_ZERO * RANK), 1.0, 6.0, ((2, 4),), jnp.float32),
        "momentum": draw_momentum(jax.random.fold_in(streams_of[9], 71), 0),
        "vec_momentum": draw_vec_momentum(jax.random.fold_in(streams_of[9], 71), 0),
        "prompt_len": draw_prompt_len(jax.random.fold_in(streams_of[9], 71), 0),
    }


@jax.custom_vjp
def low(v):
    return lax.optimization_barrier(v.astype(jnp.bfloat16)).astype(jnp.float32)

@jax.custom_vjp
def low_back(v):
    return v

def low_keep(v):
    return (low(v), None)

def low_pass(kept, grad):
    return (grad,)

def back_keep(v):
    return (v, None)

def back_low(kept, grad):
    return (low(grad),)
low.defvjp(low_keep, low_pass)
low_back.defvjp(back_keep, back_low)
EPS = 1e-06
MU = 0.9
LOG2E = 1.442695041
NEG = -1e+30
PRECISION_HIGH = lax.Precision.HIGHEST

def rms_scale(field):
    return lax.rsqrt(lax.optimization_barrier(jnp.mean(field * field, axis=-1, keepdims=True)) + EPS)

def orthonormal(factor):
    columns = []
    for col_index in range(factor.shape[-1]):
        column = factor[..., col_index]
        for earlier in columns:
            column = column - lax.optimization_barrier(jnp.sum(earlier * column, axis=-2, keepdims=True)) * earlier
        column = column * lax.rsqrt(lax.optimization_barrier(jnp.sum(column * column, axis=-2, keepdims=True)) + EPS)
        columns.append(column)
    return jnp.stack(columns, axis=-1)

def forward(tok_float, weight_float, vec_float, prompt_valid):
    gain_one = vec_float[0]
    gain_two = vec_float[1]
    bias_one = vec_float[2]
    bias_two = vec_float[3]
    scale_raw = vec_float[4]
    group_rows = tok_float.shape[0]
    normed_one = low(tok_float * rms_scale(tok_float) * gain_one)
    projected = jnp.einsum('ti,omi->mto', normed_one, weight_float[:, 0:3, :], precision=PRECISION_HIGH)
    query = low_back(projected[0])
    key_low = low(low_back(projected[1]))
    value_low = low(low_back(projected[2]))
    query_scale = LOG2E / math.sqrt(HEAD_DIM) * jax.nn.softplus(scale_raw)
    scaled = low(query * query_scale)
    k_heads = key_low.reshape(group_rows, HEADS, HEAD_DIM)
    v_heads = value_low.reshape(group_rows, HEADS, HEAD_DIM)
    k_index = jnp.arange(group_rows, dtype=jnp.int32)
    k_block = k_index // TOK_DEV
    k_offset = k_index % TOK_DEV
    k_prompt = k_offset < PROMPT_DEV
    k_pos = k_block * PROMPT_DEV + k_offset
    q_blocks = scaled.reshape(N_ZERO, TOK_DEV, HEADS, HEAD_DIM)

    def attend(block_args):
        q_block, block_id = block_args
        q_offset = jnp.arange(TOK_DEV, dtype=jnp.int32)[:, None]
        q_prompt = q_offset < PROMPT_DEV
        q_pos = block_id * PROMPT_DEV + q_offset
        see_prompt = k_prompt[None] & (k_pos[None] < prompt_valid) & (jnp.logical_not(q_prompt) | (k_pos[None] <= q_pos))
        see_cont = jnp.logical_not(k_prompt[None]) & jnp.logical_not(q_prompt) & (k_block[None] == block_id) & (k_offset[None] <= q_offset)
        allowed = see_prompt | see_cont
        raw_scores = low_back(jnp.einsum('thd,khd->htk', q_block, k_heads, precision=PRECISION_HIGH))
        masked = jnp.where(allowed[None], raw_scores, NEG)
        row_top = lax.optimization_barrier(jnp.max(masked, axis=-1, keepdims=True))
        log_total = row_top + jnp.log(lax.optimization_barrier(jnp.sum(jnp.exp(masked - row_top), axis=-1, keepdims=True)))
        probs = low(jnp.exp(masked - log_total))
        return jnp.einsum('htk,khd->thd', probs, v_heads, precision=PRECISION_HIGH).reshape(TOK_DEV, HEADS * HEAD_DIM)
    attended = lax.map(jax.checkpoint(attend), (q_blocks, jnp.arange(N_ZERO, dtype=jnp.int32)))
    attended = low(low_back(attended.reshape(group_rows, HEADS * HEAD_DIM)))
    branch = low_back(jnp.einsum('ti,oi->to', attended, weight_float[:, 3, :], precision=PRECISION_HIGH))
    hidden = tok_float + branch
    normed_two = low(hidden * rms_scale(hidden) * gain_two)
    upper = low_back(jnp.einsum('ti,oi->to', normed_two, weight_float[:, 4, :], precision=PRECISION_HIGH) + bias_one)
    activ = low(jax.nn.silu(upper))
    output = low_back(jnp.einsum('ti,oi->to', activ, weight_float[:, 5, :], precision=PRECISION_HIGH) + bias_two)
    return hidden + output

def reference(tokens, cotangent, weights, vectors, error, previous_right_factors, momentum, vec_momentum, prompt_len):
    group_rows = N_ZERO * TOK_DEV
    block_rows = D // N_ZERO
    weight_float = weights.astype(jnp.float32)
    vec_float = vectors.astype(jnp.float32)
    tok_groups = tokens.reshape(GROUPS, group_rows, D)
    cot_groups = cotangent.reshape(GROUPS, group_rows, D)
    err_groups = error.reshape(GROUPS, D, MATS, D)

    def one_group(carried, inputs):
        tok_group, cot_group, err_group, prompt_valid = inputs
        out_group, pullback = jax.vjp(lambda tok_arg, weight_arg, vec_arg: forward(tok_arg, weight_arg, vec_arg, prompt_valid), tok_group.astype(jnp.float32), weight_float, vec_float)
        grad_tok, grad_mat, grad_vec = pullback(cot_group.astype(jnp.float32))
        return (carried, (out_group.astype(jnp.bfloat16), grad_tok, grad_mat + err_group, grad_vec))
    _, (out_rows, grad_rows, combined_result, vec_grads) = lax.scan(one_group, jnp.zeros((), jnp.float32), (tok_groups, cot_groups, err_groups, prompt_len))
    blocks = combined_result.reshape(GROUPS, N_ZERO, block_rows, MATS, D)
    old_factor = previous_right_factors.reshape(MATS, D, N_ZERO, RANK).transpose(2, 0, 1, 3)
    left_mean = jnp.einsum('gzomi,zmir->zomr', blocks, old_factor, precision=PRECISION_HIGH) / N_REP
    orthogonalized = orthonormal(left_mean)
    right_mean = jnp.einsum('gzomi,zomr->zmir', blocks, orthogonalized, precision=PRECISION_HIGH) / N_REP
    approximation = jnp.einsum('zomr,zmir->zomi', orthogonalized, right_mean, precision=PRECISION_HIGH)
    new_error = (blocks - approximation[None]).reshape(GROUPS * D, MATS, D)
    grad_weights = approximation.reshape(D, MATS, D)
    fresh_right_factors = right_mean.transpose(1, 2, 0, 3).reshape(MATS, D, N_ZERO * RANK)
    step_rate = 0.03 / math.sqrt(N_ZERO * TOK_DEV)
    new_momentum = MU * momentum + grad_weights
    update_weights = -step_rate * new_momentum
    grad_vectors = lax.optimization_barrier(jnp.sum(vec_grads, axis=0)) / N_REP
    new_vec_momentum = MU * vec_momentum + grad_vectors
    update_vectors = -step_rate * new_vec_momentum
    result = out_rows.reshape(TOKENS, D)
    grad_tokens = grad_rows.reshape(TOKENS, D)
    return (result, grad_tokens, grad_weights, grad_vectors, new_error, fresh_right_factors, new_momentum, new_vec_momentum, update_weights, update_vectors)
```

```python
import math

import jax
import jax.numpy as jnp
from jax import lax
from jax.experimental import pallas as pl
from jax.experimental.pallas import tpu as pltpu
from jax.sharding import PartitionSpec as P

HEADS = 16
PROMPT = 1024
LANES = 128

EPS = 1e-06
MU = 0.9
LOG2E = 1.442695041
NEG = -1e30
PRECISION_HIGH = lax.Precision.HIGHEST
f32 = jnp.float32
bf16 = jnp.bfloat16


def rms_scale(field):
    return lax.rsqrt(jnp.mean(field * field, axis=-1, keepdims=True) + EPS)


def norm_back(field, scale, gain_vec, grad_in):
    weighted = grad_in * gain_vec
    inner = jnp.mean(field * weighted, axis=-1, keepdims=True)
    return scale * weighted - field * (scale * scale * scale) * inner


def to_pair(x, count):
    return lax.ppermute(x, "zero", [(i, i ^ 1) for i in range(count)])


def to_chip(x, count, shift):
    return lax.ppermute(x, "zero", [(i, (i + 2 * shift) % count) for i in range(count)])


def place(buffer, block, index):
    starts = (index,) + (0,) * block.ndim
    return lax.dynamic_update_slice(buffer, block[None], starts)


def gather_zero(x, index, count):
    chip, core = index // 2, index % 2
    chips = count // 2
    out = jnp.zeros((count,) + x.shape, x.dtype)
    for shift in range(chips):
        block = x if shift == 0 else to_chip(x, count, shift)
        owner = (chip - shift + chips) % chips
        out = place(out, block, owner * 2 + core)
        out = place(out, to_pair(block, count), owner * 2 + 1 - core)
    return out


def scatter_sum_zero(y, index, count, dtype):
    chip, core = index // 2, index % 2
    chips = count // 2
    paired = y.reshape((chips, 2) + y.shape[1:])
    away = lax.dynamic_index_in_dim(paired, 1 - core, 1, keepdims=False)
    mine = lax.dynamic_index_in_dim(paired, core, 1, keepdims=False)
    mine = mine.astype(f32) + to_pair(away, count).astype(f32)
    total = lax.dynamic_index_in_dim(mine, chip, 0, keepdims=False)
    for shift in range(1, chips):
        sent = lax.dynamic_index_in_dim(mine, (chip + shift) % chips, 0, keepdims=False)
        total = total + to_chip(sent.astype(dtype), count, shift).astype(f32)
    return total


def exchange_zero(y, index, count):
    chip, core = index // 2, index % 2
    chips = count // 2
    by_chip = y.reshape((chips, 2) + y.shape[1:])
    out = jnp.zeros(y.shape, y.dtype)
    for shift in range(chips):
        sent = lax.dynamic_index_in_dim(by_chip, (chip + shift) % chips, 0, keepdims=False)
        held = sent if shift == 0 else to_chip(sent, count, shift)
        source = (chip - shift + chips) % chips
        own = lax.dynamic_index_in_dim(held, core, 0, keepdims=False)
        other = lax.dynamic_index_in_dim(held, 1 - core, 0, keepdims=False)
        out = place(out, own, source * 2 + core)
        out = place(out, to_pair(other, count), source * 2 + 1 - core)
    return out


def sum_rep(x, count, dtype=f32):
    step = 1
    while step < count:
        low = x.astype(dtype)
        far = lax.ppermute(low, "rep", [(i, i ^ step) for i in range(count)])
        x = low.astype(f32) + far.astype(f32)
        step *= 2
    return x


def ortho_body(left_ref, out_ref):
    rank = left_ref.shape[0]
    columns = [left_ref[c] for c in range(rank)]
    for e in range(rank):
        done = columns[e]
        done = done * lax.rsqrt(jnp.sum(done * done, axis=-1, keepdims=True) + EPS)
        out_ref[e] = done
        for c in range(e + 1, rank):
            columns[c] = columns[c] - jnp.sum(done * columns[c], axis=-1, keepdims=True) * done


def orthonormal(left):
    return pl.pallas_call(
        ortho_body, out_shape=jax.ShapeDtypeStruct(left.shape, f32), name="ortho"
    )(left)


def on_device(
    tokens,
    cotangent,
    weights,
    vectors,
    error,
    previous_right_factors,
    momentum,
    vec_momentum,
    prompt_len,
):
    zero_index = lax.axis_index("zero")
    rep_index = lax.axis_index("rep")
    n = lax.axis_size("zero")
    rep_count = lax.axis_size("rep")
    rows, width = tokens.shape
    head_dim = width // HEADS
    heads = HEADS // n
    own = weights.shape[0]
    group_rows = n * rows
    prompt_rows = PROMPT // n
    prompt_valid = prompt_len[0]

    full_v = gather_zero(vectors, zero_index, n).transpose(1, 0, 2).reshape(5, width)
    vec_float = full_v.astype(f32)
    gain_one, gain_two, bias_one, bias_two = (vec_float[i] for i in range(4))
    scale_raw = vectors[4].astype(f32)
    far_w = gather_zero(weights[:, 3:6, :], zero_index, n).reshape(width, 3, width)

    tok_all = gather_zero(tokens, zero_index, n).reshape(group_rows, width)
    tok_all_float = tok_all.astype(f32)
    normed_all = (tok_all_float * rms_scale(tok_all_float) * gain_one).astype(bf16)

    projected = jnp.einsum(
        "ti,omi->mto", normed_all, weights[:, 0:3, :], preferred_element_type=f32
    )
    scale_const = LOG2E / math.sqrt(head_dim)
    query_scale = scale_const * jax.nn.softplus(scale_raw)
    query = projected[0]
    scaled = (query * query_scale).astype(bf16).reshape(group_rows, heads, head_dim)
    key_low = projected[1].astype(bf16).reshape(group_rows, heads, head_dim)
    value_low = projected[2].astype(bf16).reshape(group_rows, heads, head_dim)

    index = jnp.arange(group_rows, dtype=jnp.int32)
    block, offset = index // rows, index % rows
    is_prompt = offset < prompt_rows
    pos = block * prompt_rows + offset
    see_prompt = (is_prompt & (pos < prompt_valid))[None] & (
        jnp.logical_not(is_prompt)[:, None] | (pos[None] <= pos[:, None])
    )
    see_cont = (
        jnp.logical_not(is_prompt)[None]
        & jnp.logical_not(is_prompt)[:, None]
        & (block[None] == block[:, None])
        & (offset[None] <= offset[:, None])
    )
    allowed = see_prompt | see_cont

    def masked_scores():
        raw = jnp.einsum("thd,khd->htk", scaled, key_low, preferred_element_type=f32)
        return jnp.where(allowed[None], raw, NEG)

    masked = masked_scores()
    row_top = jnp.max(masked, axis=-1, keepdims=True)
    log_total = row_top + jnp.log(jnp.sum(jnp.exp(masked - row_top), axis=-1, keepdims=True))
    probs = jnp.exp(masked - log_total)
    attended_heads = jnp.einsum(
        "htk,khd->thd", probs.astype(bf16), value_low, preferred_element_type=f32
    ).astype(bf16)
    attended = (
        exchange_zero(attended_heads.reshape(n, rows, own), zero_index, n)
        .transpose(1, 0, 2)
        .reshape(rows, width)
    )

    tok_float = tokens.astype(f32)
    scale_one = rms_scale(tok_float)
    hidden = tok_float + jnp.einsum("ti,oi->to", attended, far_w[:, 0], preferred_element_type=f32)
    scale_two = rms_scale(hidden)
    normed_two = (hidden * scale_two * gain_two).astype(bf16)
    upper = (
        jnp.einsum("ti,oi->to", normed_two, far_w[:, 1], preferred_element_type=f32) + bias_one
    )
    activ = jax.nn.silu(upper).astype(bf16)
    output = jnp.einsum("ti,oi->to", activ, far_w[:, 2], preferred_element_type=f32) + bias_two
    result = (hidden + output).astype(bf16)

    grad_out = cotangent.astype(f32)
    grad_f = cotangent.astype(bf16)
    grad_act = jnp.einsum("to,oi->ti", grad_f, far_w[:, 2], preferred_element_type=f32)
    gate_sig = jax.nn.sigmoid(upper)
    grad_up = (grad_act * gate_sig * (1.0 + upper * (1.0 - gate_sig))).astype(bf16)
    grad_n2 = jnp.einsum("to,oi->ti", grad_up, far_w[:, 1], preferred_element_type=f32)
    grad_gain_two = jnp.sum(grad_n2 * hidden * scale_two, axis=0)
    grad_hidden = grad_out + norm_back(hidden, scale_two, gain_two, grad_n2)
    grad_branch = grad_hidden.astype(bf16)
    grad_att = jnp.einsum(
        "to,oi->ti", grad_branch, far_w[:, 0], preferred_element_type=f32
    ).astype(bf16)
    grad_att_heads = exchange_zero(
        grad_att.reshape(rows, n, own).transpose(1, 0, 2), zero_index, n
    ).reshape(group_rows, heads, head_dim)

    far_grads = jnp.einsum(
        "mto,mti->omi",
        jnp.stack([grad_branch, grad_up, grad_f], axis=0),
        jnp.stack([attended, normed_two, activ], axis=0),
        preferred_element_type=f32,
    ).astype(bf16)
    far_block = scatter_sum_zero(far_grads.reshape(n, own, 3, width), zero_index, n, bf16)

    probs_again = jnp.exp(masked_scores() - log_total)
    grad_probs = jnp.einsum("thd,khd->htk", grad_att_heads, value_low, preferred_element_type=f32)
    delta = jnp.sum(probs_again * grad_probs, axis=-1, keepdims=True)
    grad_scores = (probs_again * (grad_probs - delta)).astype(bf16)
    grad_value = jnp.einsum(
        "htk,thd->khd", probs_again.astype(bf16), grad_att_heads, preferred_element_type=f32
    ).reshape(group_rows, own)
    grad_key = jnp.einsum(
        "htk,thd->khd", grad_scores, scaled, preferred_element_type=f32
    ).reshape(group_rows, own)
    grad_sq = jnp.einsum("htk,khd->thd", grad_scores, key_low, preferred_element_type=f32).reshape(
        group_rows, own
    )
    grad_query = grad_sq * query_scale
    grad_proj = jnp.stack([grad_query, grad_key, grad_value], axis=0).astype(bf16)
    near_block = jnp.einsum("mto,ti->omi", grad_proj, normed_all, preferred_element_type=f32)
    grad_n1_part = jnp.einsum(
        "mto,omi->ti", grad_proj, weights[:, 0:3, :], preferred_element_type=f32
    ).astype(bf16)
    grad_n1 = scatter_sum_zero(grad_n1_part.reshape(n, rows, width), zero_index, n, bf16)
    grad_tokens = grad_hidden + norm_back(tok_float, scale_one, gain_one, grad_n1)

    grad_scale_raw = jnp.sum(grad_sq * query, axis=0) * scale_const * jax.nn.sigmoid(scale_raw)
    vec_terms = jnp.stack(
        [
            jnp.sum(grad_n1 * tok_float * scale_one, axis=0),
            grad_gain_two,
            jnp.sum(grad_up.astype(f32), axis=0),
            jnp.sum(grad_f.astype(f32), axis=0),
        ],
        axis=0,
    )
    vec_block = scatter_sum_zero(
        vec_terms.reshape(4, n, own).transpose(1, 0, 2), zero_index, n, f32
    )
    vec_total = sum_rep(jnp.concatenate([vec_block, grad_scale_raw[None]], axis=0), rep_count)

    merged = jnp.concatenate([near_block, far_block], axis=1) + error
    left = jnp.einsum("omi,mir->rmo", merged, previous_right_factors, precision=PRECISION_HIGH)
    ortho = orthonormal(sum_rep(left, rep_count) / rep_count)
    right = jnp.einsum("omi,rmo->rmi", merged, ortho, precision=PRECISION_HIGH)
    right = sum_rep(right, rep_count, bf16) / rep_count
    fresh_right_factors = right.transpose(1, 2, 0)
    approximation = jnp.einsum("rmo,rmi->omi", ortho, right, precision=PRECISION_HIGH)
    new_error = merged - approximation

    rep_width = width // rep_count
    grad_weights = lax.dynamic_slice_in_dim(approximation, rep_index * rep_width, rep_width, 2)
    step_rate = 0.03 / math.sqrt(group_rows)
    new_momentum = MU * momentum + grad_weights
    update_weights = -step_rate * new_momentum
    grad_vectors = vec_total / rep_count
    new_vec_momentum = MU * vec_momentum + grad_vectors
    update_vectors = -step_rate * new_vec_momentum
    return (
        result,
        grad_tokens,
        grad_weights,
        grad_vectors,
        new_error,
        fresh_right_factors,
        new_momentum,
        new_vec_momentum,
        update_weights,
        update_vectors,
    )


def solution(mesh):
    in_specs = (
        P(("rep", "zero"), None),
        P(("rep", "zero"), None),
        P("zero", None, None),
        P(None, "zero"),
        P(("rep", "zero"), None, None),
        P(None, None, "zero"),
        P("zero", None, "rep"),
        P(None, "zero"),
        P("rep"),
    )
    out_specs = (
        P(("rep", "zero"), None),
        P(("rep", "zero"), None),
        P("zero", None, "rep"),
        P(None, "zero"),
        P(("rep", "zero"), None, None),
        P(None, None, "zero"),
        P("zero", None, "rep"),
        P(None, "zero"),
        P("zero", None, "rep"),
        P(None, "zero"),
    )
    return jax.shard_map(
        on_device, mesh=mesh, in_specs=in_specs, out_specs=out_specs, check_vma=False
    )
```

```python
import math

import jax
import jax.numpy as jnp
from jax import lax
from jax.experimental import pallas as pl
from jax.experimental.pallas import tpu as pltpu
from jax.sharding import PartitionSpec as P

HEADS = 16
PROMPT = 1024
LANES = 128

EPS = 1e-06
MU = 0.9
LOG2E = 1.442695041
NEG = -1e30
PRECISION_HIGH = lax.Precision.HIGHEST
f32 = jnp.float32
bf16 = jnp.bfloat16


def rms_scale(field):
    return lax.rsqrt(jnp.mean(field * field, axis=-1, keepdims=True) + EPS)


def norm_back(field, scale, gain_vec, grad_in):
    weighted = grad_in * gain_vec
    inner = jnp.mean(field * weighted, axis=-1, keepdims=True)
    return scale * weighted - field * (scale * scale * scale) * inner


def to_pair(x, count):
    return lax.ppermute(x, "zero", [(i, i ^ 1) for i in range(count)])


def to_chip(x, count, shift):
    return lax.ppermute(x, "zero", [(i, (i + 2 * shift) % count) for i in range(count)])


def relative(index, count):
    chips = count // 2
    chip, core = index // 2, index % 2
    shift, flip = jnp.arange(count) // 2, jnp.arange(count) % 2
    sources = ((chip - shift + chips) % chips) * 2 + (core ^ flip)
    receivers = ((chip + shift) % chips) * 2 + (core ^ flip)
    owner = jnp.arange(count)
    places = ((owner // 2 - chip + chips) % chips) * 2 + ((owner % 2) ^ core)
    return tuple(a.astype(jnp.int32) for a in (sources, receivers, places))


def gather_zero(x, count):
    out = []
    for shift in range(count // 2):
        block = x if shift == 0 else to_chip(x, count, shift)
        out += [block, to_pair(block, count)]
    return out


def exchange_zero(y, count):
    out = []
    for shift in range(count // 2):
        held = y[2 * shift : 2 * shift + 2]
        if shift:
            held = to_chip(held, count, shift)
        out += [held[0], to_pair(held[1], count)]
    return out


def scatter_sum_zero(mine, away, count):
    held = mine.astype(f32) + to_pair(away, count).astype(f32)
    terms = [held[0]]
    for shift in range(1, count // 2):
        terms.append(to_chip(held[shift].astype(mine.dtype), count, shift).astype(f32))
    return terms


def sum_rep(x, count, dtype=f32):
    step = 1
    while step < count:
        low = x.astype(dtype)
        far = lax.ppermute(low, "rep", [(i, i ^ step) for i in range(count)])
        x = low.astype(f32) + far.astype(f32)
        step *= 2
    return x


def dot(a, b, dims):
    return lax.dot_general(a, b, (dims, ((), ())), preferred_element_type=f32)


NN = ((1,), (0,))
NT = ((1,), (1,))
TN = ((0,), (0,))
ANY = pl.BlockSpec(memory_space=pl.ANY)
VMEM_LIMIT = 60 * 1024 * 1024


def params(steps=1):
    return pltpu.CompilerParams(
        dimension_semantics=("arbitrary",) * steps, vmem_limit_bytes=VMEM_LIMIT
    )


def cost(flops, moved):
    return pl.CostEstimate(flops=int(flops), bytes_accessed=int(moved), transcendentals=0)


def project_body(index_ref, tok_a, tok_b, gain_ref, w_ref, scale_ref, *refs):
    normed_ref, qkv_ref, query_ref = refs[-3:]
    step = pl.program_id(0)
    tok = jnp.where(step == 0, tok_a[...], tok_b[...]).astype(f32)
    normed = (tok * rms_scale(tok) * gain_ref[...]).astype(bf16)
    normed_ref[0] = normed
    own = w_ref.shape[1]
    query = dot(w_ref[0], normed, NT)
    query_ref[0] = query.astype(bf16)
    qkv_ref[0, 0:own] = (query * scale_ref[...]).astype(bf16)
    qkv_ref[0, own : 2 * own] = dot(w_ref[1], normed, NT).astype(bf16)
    qkv_ref[0, 2 * own :] = dot(w_ref[2], normed, NT).astype(bf16)


def project(owners, tok_a, tok_b, gain, w_mats, query_scale, count, held):
    rows, width = tok_a.shape
    own = w_mats.shape[1]
    shapes = (
        jax.ShapeDtypeStruct((count, rows, width), bf16),
        jax.ShapeDtypeStruct((count, 3 * own, rows), bf16),
        jax.ShapeDtypeStruct((count, own, rows), bf16),
    )
    whole = lambda *shape: pl.BlockSpec(shape, lambda s, at: (0,) * len(shape))
    held = () if held is None else tuple(held)
    return pl.pallas_call(
        project_body,
        out_shape=shapes,
        grid_spec=pltpu.PrefetchScalarGridSpec(
            num_scalar_prefetch=1,
            grid=(2,),
            in_specs=[
                whole(rows, width),
                whole(rows, width),
                whole(1, width),
                whole(3, own, width),
                whole(own, 1),
            ]
            + [ANY] * len(held),
            out_specs=[
                pl.BlockSpec((1, rows, width), lambda s, at: (at[s], 0, 0)),
                pl.BlockSpec((1, 3 * own, rows), lambda s, at: (at[s], 0, 0)),
                pl.BlockSpec((1, own, rows), lambda s, at: (at[s], 0, 0)),
            ],
        ),
        input_output_aliases={6 + i: i for i in range(len(held))},
        compiler_params=params(),
        cost_estimate=cost(2 * 2 * rows * 3 * own * width, 3 * own * width * 2 + 8 * rows * width),
        name="project",
    )(owners, tok_a, tok_b, gain, w_mats, query_scale, *held)


def masked_chunks(raw, size, diagonal, valid):
    chunks = []
    for j in range(raw.shape[0] // size):
        part = raw[j * size : (j + 1) * size]
        allowed = None
        if (j + 1) * size > PROMPT // 2:
            at = j * size + lax.broadcasted_iota(jnp.int32, part.shape, 0)
            allowed = at < valid
        if j == diagonal:
            causal = lax.broadcasted_iota(jnp.int32, part.shape, 0) <= lax.broadcasted_iota(
                jnp.int32, part.shape, 1
            )
            allowed = causal if allowed is None else allowed & causal
        chunks.append((part, allowed))
    return chunks


def units_of(count, prompt_rows, rows):
    for b in range(count):
        yield b, slice(0, prompt_rows), (b + 1) * prompt_rows, b, False
        yield b, slice(prompt_rows, rows), count * prompt_rows, None, True


def attend_body(valid_ref, place_ref, q_ref, k_ref, v_ref, att_ref, lse_ref, keys, values):
    count, _, rows = q_ref.shape
    size = PROMPT // count
    valid = valid_ref[0]
    for j in range(count):
        keys[j * size : (j + 1) * size, :] = k_ref[j, :, :size].T
        values[:, j * size : (j + 1) * size] = v_ref[j, :, :size]
    for b, lanes, seen, diagonal, own_cont in units_of(count, size, rows):
        query = q_ref[b, :, lanes]
        chunks = masked_chunks(dot(keys[:seen], query, NN), size, diagonal, valid)
        if own_cont:
            raw = dot(k_ref[b, :, size:].T, query, NN)
            chunks += masked_chunks(raw, raw.shape[0], 0, raw.shape[0])
        chunks = [p if ok is None else jnp.where(ok, p, NEG) for p, ok in chunks]
        top = chunks[0].max(axis=0, keepdims=True)
        for part in chunks[1:]:
            top = jnp.maximum(top, part.max(axis=0, keepdims=True))
        chunks = [jnp.exp(part - top) for part in chunks]
        total = chunks[0].sum(axis=0, keepdims=True)
        for part in chunks[1:]:
            total = total + part.sum(axis=0, keepdims=True)
        attended = None
        for j, part in enumerate(chunks):
            v_part = values[:, j * size : (j + 1) * size] if j * size < seen else v_ref[b, :, size:]
            term = dot(v_part, part.astype(bf16), NN)
            attended = term if attended is None else attended + term
        att_ref[place_ref[b], :, lanes] = (attended / total).astype(bf16)
        lse_ref[0, b : b + 1, lanes] = top + jnp.log(total)


def attend(valid, places, qkv, heads, head_dim):
    count, three_own, rows = qkv.shape
    own = three_own // 3
    block = lambda kind: pl.BlockSpec(
        (count, head_dim, rows), lambda h, *_: (0, kind * heads + h, 0)
    )
    pairs = PROMPT * PROMPT // 2 + PROMPT * count * (rows - PROMPT // count)
    return pl.pallas_call(
        attend_body,
        out_shape=(
            jax.ShapeDtypeStruct((count, own, rows), bf16),
            jax.ShapeDtypeStruct((heads, count, rows), f32),
        ),
        grid_spec=pltpu.PrefetchScalarGridSpec(
            num_scalar_prefetch=2,
            grid=(heads,),
            in_specs=[block(0), block(1), block(2)],
            out_specs=[
                pl.BlockSpec((count, head_dim, rows), lambda h, *_: (0, h, 0)),
                pl.BlockSpec((1, count, rows), lambda h, *_: (h, 0, 0)),
            ],
            scratch_shapes=[
                pltpu.VMEM((PROMPT, head_dim), bf16),
                pltpu.VMEM((head_dim, PROMPT), bf16),
            ],
        ),
        compiler_params=params(),
        cost_estimate=cost(4 * 256 * heads * pairs, qkv.size * 3),
        name="attend",
    )(valid, places, qkv, qkv, qkv)


def attend_back_body(
    valid_ref, place_ref, q_ref, k_ref, v_ref, query_ref, att_ref, lse_ref, scale_ref, *refs
):
    count, head_dim, rows = q_ref.shape
    parts = refs[:count]
    grad_ref, sum_ref, keys, values, grad_keys, grad_values, grad_att = refs[count:]
    size = PROMPT // count
    valid = valid_ref[0]
    for i in range(count):
        grad_att[place_ref[count + i]] = parts[i][...]
    for j in range(count):
        keys[j * size : (j + 1) * size, :] = k_ref[j, :, :size].T
        values[j * size : (j + 1) * size, :] = v_ref[j, :, :size].T
    grad_keys[...] = jnp.zeros_like(grad_keys)
    grad_values[...] = jnp.zeros_like(grad_values)
    scale_sum = jnp.zeros((head_dim, 1), f32)
    for b, lanes, seen, diagonal, own_cont in units_of(count, size, rows):
        query = q_ref[b, :, lanes]
        grad_out = grad_att[b, :, lanes]
        query_rows = query.T
        grad_rows = grad_out.T
        lse = lse_ref[0, b : b + 1, lanes]
        delta = jnp.sum(
            att_ref[place_ref[b], :, lanes].astype(f32) * grad_out.astype(f32),
            axis=0,
            keepdims=True,
        )
        grad_query = jnp.zeros(query.shape, f32)

        def block(key_rows, value_rows, chunk_size, diag, limit):
            raw = dot(key_rows, query, NN)
            grad_probs = dot(value_rows, grad_out, NN)
            probs, scores = [], []
            for j, (part, ok) in enumerate(masked_chunks(raw, chunk_size, diag, limit)):
                prob = jnp.exp(part - lse)
                if ok is not None:
                    prob = jnp.where(ok, prob, 0.0)
                score = prob * (grad_probs[j * chunk_size : (j + 1) * chunk_size] - delta)
                probs.append(prob.astype(bf16))
                scores.append(score.astype(bf16))
            return probs, scores

        probs, scores = block(keys[:seen], values[:seen], size, diagonal, valid)
        for j in range(len(probs)):
            at = slice(j * size, (j + 1) * size)
            grad_values[at, :] += dot(probs[j], grad_rows, NN)
            grad_keys[at, :] += dot(scores[j], query_rows, NN)
            grad_query += dot(k_ref[j, :, :size], scores[j], NN)
        if own_cont:
            probs, scores = block(
                k_ref[b, :, size:].T, v_ref[b, :, size:].T, rows - size, 0, rows - size
            )
            grad_query += dot(k_ref[b, :, size:], scores[0], NN)
            grad_ref[1, b, :, size:] = dot(scores[0], query_rows, NN).T.astype(bf16)
            grad_ref[2, b, :, size:] = dot(probs[0], grad_rows, NN).T.astype(bf16)
        scale_sum += jnp.sum(
            grad_query * query_ref[b, :, lanes].astype(f32), axis=1, keepdims=True
        )
        grad_ref[0, b, :, lanes] = (grad_query * scale_ref[:, 0:1]).astype(bf16)
    for j in range(count):
        at = slice(j * size, (j + 1) * size)
        grad_ref[1, j, :, :size] = grad_keys[at, :].T.astype(bf16)
        grad_ref[2, j, :, :size] = grad_values[at, :].T.astype(bf16)
    sum_ref[...] = jnp.broadcast_to(scale_sum, sum_ref.shape)


def attend_back(valid, places, qkv, query, att, lse, query_scale, parts, heads, head_dim):
    count, three_own, rows = qkv.shape
    own = three_own // 3
    size = PROMPT // count
    block = lambda kind: pl.BlockSpec(
        (count, head_dim, rows), lambda h, *_: (0, kind * heads + h, 0)
    )
    pairs = PROMPT * PROMPT // 2 + PROMPT * count * (rows - size)
    return pl.pallas_call(
        attend_back_body,
        out_shape=(
            jax.ShapeDtypeStruct((3, count, own, rows), bf16),
            jax.ShapeDtypeStruct((own, LANES), f32),
        ),
        grid_spec=pltpu.PrefetchScalarGridSpec(
            num_scalar_prefetch=2,
            grid=(heads,),
            in_specs=[
                block(0),
                block(1),
                block(2),
                block(0),
                block(0),
                pl.BlockSpec((1, count, rows), lambda h, *_: (h, 0, 0)),
                pl.BlockSpec((head_dim, 1), lambda h, *_: (h, 0)),
            ]
            + [pl.BlockSpec((head_dim, rows), lambda h, *_: (h, 0))] * count,
            out_specs=[
                pl.BlockSpec((3, count, head_dim, rows), lambda h, *_: (0, 0, h, 0)),
                pl.BlockSpec((head_dim, LANES), lambda h, *_: (h, 0)),
            ],
            scratch_shapes=[
                pltpu.VMEM((PROMPT, head_dim), bf16),
                pltpu.VMEM((PROMPT, head_dim), bf16),
                pltpu.VMEM((PROMPT, head_dim), f32),
                pltpu.VMEM((PROMPT, head_dim), f32),
                pltpu.VMEM((count, head_dim, rows), bf16),
            ],
        ),
        compiler_params=params(),
        cost_estimate=cost(10 * 256 * heads * pairs, qkv.size * 5),
        name="attend_back",
    )(valid, places, qkv, qkv, qkv, query, att, lse, query_scale, *parts)


def feed_body(place_ref, tok_ref, cot_ref, vec_ref, *refs):
    count = place_ref.shape[0] // 2
    att_parts, w_parts = refs[:count], refs[count : 2 * count]
    (
        result_ref,
        hidden_grad_ref,
        att_grad_ref,
        inputs_ref,
        grads_ref,
        sums_ref,
        w,
        att,
        hidden,
        slope,
        weighted,
        turned,
        att_sems,
        w_sems,
    ) = refs[2 * count :]
    rows, width = tok_ref.shape
    own = width // count
    tile = 2 * LANES
    tiles = width // tile
    copies = []
    for i in range(count):
        at = place_ref[count + i]
        copies.append(pltpu.make_async_copy(att_parts[i], att.at[at], att_sems.at[i]))
        copies[-1].start()
    w_copies = [[], [], []]
    for m in range(3):
        for i in range(count):
            at = place_ref[count + i]
            one = pltpu.make_async_copy(w_parts[i].at[m], w.at[m, at], w_sems.at[m, i])
            one.start()
            w_copies[m].append(one)
    for one in copies:
        one.wait()
    attended = att[...].reshape(width, rows).T
    inputs_ref[0] = attended
    grad_f = cot_ref[...]
    grads_ref[2] = grad_f.T

    def w_rows(m, j):
        return w.at[m].reshape(width, width)[pl.ds(pl.multiple_of(j * tile, tile), tile), :]

    def w_cols(m, j):
        return w.at[m].reshape(width, width)[:, pl.ds(pl.multiple_of(j * tile, tile), tile)]

    def lanes(j):
        return pl.ds(pl.multiple_of(j * tile, tile), tile)

    for one in w_copies[0]:
        one.wait()

    def first(j, square):
        part = tok_ref[:, lanes(j)].astype(f32) + dot(attended, w_rows(0, j), NT)
        hidden[:, lanes(j)] = part
        return square + jnp.sum(part * part, axis=-1, keepdims=True)

    square = lax.fori_loop(0, tiles, first, jnp.zeros((rows, 1), f32))
    scale = lax.rsqrt(square / width + EPS)
    normed = (hidden[...] * scale * vec_ref[1:2, :]).astype(bf16)
    inputs_ref[1] = normed
    for m in (1, 2):
        for one in w_copies[m]:
            one.wait()

    def second(j, carry):
        upper = dot(normed, w_rows(1, j), NT) + vec_ref[2:3, lanes(j)]
        gate = 1.0 / (1.0 + jnp.exp(-upper))
        inputs_ref[2, :, lanes(j)] = (upper * gate).astype(bf16)
        grad_act = dot(grad_f, w_cols(2, j), NN)
        grad_up = (grad_act * gate * (1.0 + upper * (1.0 - gate))).astype(bf16)
        slope[:, lanes(j)] = grad_up
        sums_ref[1:2, lanes(j)] = jnp.sum(grad_up.astype(f32), axis=0, keepdims=True)
        sums_ref[2:3, lanes(j)] = jnp.sum(
            cot_ref[:, lanes(j)].astype(f32), axis=0, keepdims=True
        )
        return carry

    lax.fori_loop(0, tiles, second, 0)
    grad_up = slope[...]
    grads_ref[1] = grad_up.T
    activ = inputs_ref[2]

    def third(j, inner):
        part = hidden[:, lanes(j)]
        out = dot(activ, w_rows(2, j), NT) + vec_ref[3:4, lanes(j)]
        result_ref[:, lanes(j)] = (part + out).astype(bf16)
        grad_normed = dot(grad_up, w_cols(1, j), NN)
        sums_ref[0:1, lanes(j)] = jnp.sum(grad_normed * part * scale, axis=0, keepdims=True)
        turn = grad_normed * vec_ref[1:2, lanes(j)]
        weighted[:, lanes(j)] = turn
        return inner + jnp.sum(part * turn, axis=-1, keepdims=True)

    inner = lax.fori_loop(0, tiles, third, jnp.zeros((rows, 1), f32)) / width
    back = cot_ref[...].astype(f32) + (
        scale * weighted[...] - hidden[...] * (scale * scale * scale) * inner
    )
    hidden_grad_ref[...] = back
    branch = back.astype(bf16)
    grads_ref[0] = branch.T

    def fourth(j, carry):
        turned[lanes(j), :] = dot(branch, w_cols(0, j), NN).astype(bf16).T
        return carry

    lax.fori_loop(0, tiles, fourth, 0)
    for i in range(count):
        att_grad_ref[place_ref[i]] = turned[i * own : (i + 1) * own, :]


def feed(places, tokens, cotangent, vec, att_parts, w_parts):
    count = len(att_parts)
    rows, width = tokens.shape
    own = width // count
    whole = lambda *shape: pl.BlockSpec(shape, lambda i, at: (0,) * len(shape))
    return pl.pallas_call(
        feed_body,
        out_shape=(
            jax.ShapeDtypeStruct((rows, width), bf16),
            jax.ShapeDtypeStruct((rows, width), f32),
            jax.ShapeDtypeStruct((count, own, rows), bf16),
            jax.ShapeDtypeStruct((3, rows, width), bf16),
            jax.ShapeDtypeStruct((3, width, rows), bf16),
            jax.ShapeDtypeStruct((8, width), f32),
        ),
        grid_spec=pltpu.PrefetchScalarGridSpec(
            num_scalar_prefetch=1,
            grid=(1,),
            in_specs=[whole(rows, width), whole(rows, width), whole(*vec.shape)]
            + [ANY] * (2 * count),
            out_specs=[
                whole(rows, width),
                whole(rows, width),
                whole(count, own, rows),
                whole(3, rows, width),
                whole(3, width, rows),
                whole(8, width),
            ],
            scratch_shapes=[
                pltpu.VMEM((3, count, own, width), bf16),
                pltpu.VMEM((count, own, rows), bf16),
                pltpu.VMEM((rows, width), f32),
                pltpu.VMEM((rows, width), bf16),
                pltpu.VMEM((rows, width), f32),
                pltpu.VMEM((width, rows), bf16),
                pltpu.SemaphoreType.DMA((count,)),
                pltpu.SemaphoreType.DMA((3, count)),
            ],
        ),
        compiler_params=params(),
        cost_estimate=cost(12 * rows * width * width, 3 * width * width * 2 + rows * width * 24),
        name="feed",
    )(places, tokens, cotangent, vec, *att_parts, *w_parts)


def outer_body(order_ref, grad_ref, input_ref, out_ref):
    out_ref[0, 0] = dot(grad_ref[0, 0], input_ref[0], NN).astype(bf16)


def outer(order, grads, inputs):
    mats, width, rows = grads.shape
    blocks = order.shape[0]
    count = lax.axis_size("zero")
    own = width // count
    return pl.pallas_call(
        outer_body,
        out_shape=jax.ShapeDtypeStruct((blocks, mats, own, width), bf16),
        grid_spec=pltpu.PrefetchScalarGridSpec(
            num_scalar_prefetch=1,
            grid=(blocks, mats),
            in_specs=[
                pl.BlockSpec((1, 1, own, rows), lambda s, m, at: (m, at[s], 0, 0)),
                pl.BlockSpec((1, rows, width), lambda s, m, at: (m, 0, 0)),
            ],
            out_specs=pl.BlockSpec((1, 1, own, width), lambda s, m, at: (s, m, 0, 0)),
        ),
        compiler_params=params(2),
        cost_estimate=cost(2 * blocks * mats * own * width * rows, blocks * mats * own * width * 4),
        name="outer",
    )(order, grads.reshape(mats, count, own, rows), inputs)


def ortho_body(left_ref, out_ref):
    rank = left_ref.shape[0]
    columns = [left_ref[c] for c in range(rank)]
    for e in range(rank):
        done = columns[e]
        done = done * lax.rsqrt(jnp.sum(done * done, axis=-1, keepdims=True) + EPS)
        out_ref[e] = done
        for c in range(e + 1, rank):
            columns[c] = columns[c] - jnp.sum(done * columns[c], axis=-1, keepdims=True) * done


def orthonormal(left):
    return pl.pallas_call(
        ortho_body, out_shape=jax.ShapeDtypeStruct(left.shape, f32), name="ortho"
    )(left)


def on_device(
    tokens,
    cotangent,
    weights,
    vectors,
    error,
    previous_right_factors,
    momentum,
    vec_momentum,
    prompt_len,
):
    zero_index = lax.axis_index("zero")
    rep_index = lax.axis_index("rep")
    n = lax.axis_size("zero")
    rep_count = lax.axis_size("rep")
    rows, width = tokens.shape
    head_dim = width // HEADS
    heads = HEADS // n
    own = weights.shape[0]
    group_rows = n * rows
    sources, receivers, places = relative(zero_index, n)
    maps = jnp.concatenate([places, sources])
    w_mats = weights.transpose(1, 0, 2)

    tok_parts = gather_zero(tokens, n)
    vec_parts = gather_zero(vectors, n)
    full_v = jnp.zeros((n,) + vectors.shape, bf16)
    for i in range(n):
        full_v = lax.dynamic_update_slice(full_v, vec_parts[i][None], (sources[i], 0, 0))
    vec_float = full_v.transpose(1, 0, 2).reshape(-1, width).astype(f32)
    far_parts = gather_zero(w_mats[3:6], n)

    scale_raw = vectors[4].astype(f32)
    scale_const = LOG2E / math.sqrt(head_dim)
    query_scale = (scale_const * jax.nn.softplus(scale_raw)).reshape(own, 1)
    held = None
    for s in range(n // 2):
        held = project(
            sources[2 * s : 2 * s + 2],
            tok_parts[2 * s],
            tok_parts[2 * s + 1],
            vec_float[0:1],
            w_mats,
            query_scale,
            n,
            held,
        )
    normed_all, qkv, query = held
    att_heads, lse = attend(prompt_len, places, qkv, heads, head_dim)
    att_parts = exchange_zero(att_heads, n)
    result, grad_hidden, att_grad, far_inputs, far_grads, sums = feed(
        maps, tokens, cotangent, vec_float, att_parts, far_parts
    )
    grad_parts = exchange_zero(att_grad, n)
    away = outer(receivers[1::2], far_grads, far_inputs)
    mine = outer(receivers[0::2], far_grads, far_inputs)
    far_terms = scatter_sum_zero(mine, away, n)

    grads, scale_sums = attend_back(
        prompt_len, maps, qkv, query, att_heads, lse, query_scale, grad_parts, heads, head_dim
    )
    near_block = jnp.einsum("mbot,bti->moi", grads, normed_all, preferred_element_type=f32)
    grad_n1_part = jnp.einsum(
        "mbot,moi->bti", grads, w_mats[0:3], preferred_element_type=f32
    ).astype(bf16)
    part_of = lambda at: lax.dynamic_index_in_dim(grad_n1_part, at, 0, keepdims=False)
    n1_terms = scatter_sum_zero(
        jnp.stack([part_of(receivers[i]) for i in range(0, n, 2)]),
        jnp.stack([part_of(receivers[i]) for i in range(1, n, 2)]),
        n,
    )
    grad_n1 = sum(n1_terms[1:], n1_terms[0])
    tok_float = tokens.astype(f32)
    scale_one = rms_scale(tok_float)
    gain_one = vec_float[0]
    grad_tokens = grad_hidden + norm_back(tok_float, scale_one, gain_one, grad_n1)

    grad_scale_raw = scale_sums[:, 0] * scale_const * jax.nn.sigmoid(scale_raw)
    vec_terms = jnp.concatenate(
        [jnp.sum(grad_n1 * tok_float * scale_one, axis=0)[None], sums[0:3]], axis=0
    )
    vec_blocks = vec_terms.reshape(4, n, own).transpose(1, 0, 2)
    vec_of = lambda at: lax.dynamic_index_in_dim(vec_blocks, at, 0, keepdims=False)
    vec_block = sum(
        scatter_sum_zero(
            jnp.stack([vec_of(receivers[i]) for i in range(0, n, 2)]),
            jnp.stack([vec_of(receivers[i]) for i in range(1, n, 2)]),
            n,
        )
    )
    vec_total = sum_rep(jnp.concatenate([vec_block, grad_scale_raw[None]], axis=0), rep_count)

    far_block = sum(far_terms[1:], far_terms[0])
    merged = jnp.concatenate([near_block, far_block], axis=0) + error.transpose(1, 0, 2)
    old_right = previous_right_factors.transpose(0, 2, 1)
    left = jnp.einsum("moi,mri->rmo", merged, old_right, precision=PRECISION_HIGH)
    ortho = orthonormal(sum_rep(left, rep_count) / rep_count)
    right = jnp.einsum("moi,rmo->mri", merged, ortho, precision=PRECISION_HIGH)
    right = sum_rep(right, rep_count, bf16) / rep_count
    fresh_right_factors = right.transpose(0, 2, 1)
    approximation = jnp.einsum("rmo,mri->moi", ortho, right, precision=PRECISION_HIGH)
    new_error = (merged - approximation).transpose(1, 0, 2)

    rep_width = width // rep_count
    own_right = lax.dynamic_slice_in_dim(right, rep_index * rep_width, rep_width, 2)
    own_grads = jnp.einsum("mri,rmo->mio", own_right, ortho, precision=PRECISION_HIGH)
    step_rate = 0.03 / math.sqrt(group_rows)
    own_momentum = MU * momentum.transpose(1, 2, 0) + own_grads
    grad_weights = own_grads.transpose(2, 0, 1)
    new_momentum = own_momentum.transpose(2, 0, 1)
    update_weights = (-step_rate * own_momentum).transpose(2, 0, 1)
    grad_vectors = vec_total / rep_count
    new_vec_momentum = MU * vec_momentum + grad_vectors
    update_vectors = -step_rate * new_vec_momentum
    return (
        result,
        grad_tokens,
        grad_weights,
        grad_vectors,
        new_error,
        fresh_right_factors,
        new_momentum,
        new_vec_momentum,
        update_weights,
        update_vectors,
    )


def solution(mesh):
    in_specs = (
        P(("rep", "zero"), None),
        P(("rep", "zero"), None),
        P("zero", None, None),
        P(None, "zero"),
        P(("rep", "zero"), None, None),
        P(None, None, "zero"),
        P("zero", None, "rep"),
        P(None, "zero"),
        P("rep"),
    )
    out_specs = (
        P(("rep", "zero"), None),
        P(("rep", "zero"), None),
        P("zero", None, "rep"),
        P(None, "zero"),
        P(("rep", "zero"), None, None),
        P(None, None, "zero"),
        P("zero", None, "rep"),
        P(None, "zero"),
        P("zero", None, "rep"),
        P(None, "zero"),
    )
    return jax.shard_map(
        on_device, mesh=mesh, in_specs=in_specs, out_specs=out_specs, check_vma=False
    )
```

```python
import math

import jax
import jax.numpy as jnp
from jax import lax
from jax.experimental import pallas as pl
from jax.experimental.pallas import tpu as pltpu
from jax.sharding import PartitionSpec as P


HEADS = 16
PROMPT = 1024
LANES = 128

EPS = 1e-06
MU = 0.9
LOG2E = 1.442695041
NEG = -1e30
PRECISION_HIGH = lax.Precision.HIGHEST
f32 = jnp.float32
bf16 = jnp.bfloat16


def rms_scale(field):
    return lax.rsqrt(jnp.mean(field * field, axis=-1, keepdims=True) + EPS)


def norm_back(field, scale, gain_vec, grad_in):
    weighted = grad_in * gain_vec
    inner = jnp.mean(field * weighted, axis=-1, keepdims=True)
    return scale * weighted - field * (scale * scale * scale) * inner


def to_pair(x, count):
    return lax.ppermute(x, "zero", [(i, i ^ 1) for i in range(count)])


def to_chip(x, count, shift):
    return lax.ppermute(x, "zero", [(i, (i + 2 * shift) % count) for i in range(count)])


def to_rep(x, count, step):
    return lax.ppermute(x, "rep", [(i, i ^ step) for i in range(count)])


def relative(index, count):
    chips = count // 2
    chip, core = index // 2, index % 2
    shift, flip = jnp.arange(count) // 2, jnp.arange(count) % 2
    sources = ((chip - shift + chips) % chips) * 2 + (core ^ flip)
    receivers = ((chip + shift) % chips) * 2 + (core ^ flip)
    owner = jnp.arange(count)
    places = ((owner // 2 - chip + chips) % chips) * 2 + ((owner % 2) ^ core)
    return tuple(a.astype(jnp.int32) for a in (sources, receivers, places))


def gather_zero(x, count):
    out = []
    for shift in range(count // 2):
        block = x if shift == 0 else to_chip(x, count, shift)
        out += [block, to_pair(block, count)]
    return out


def gather_weights(w_mats, count, rep_index, rep_count):
    own = w_mats.shape[1]
    quarter = (rep_index % 4).astype(jnp.int32)
    piece = lax.dynamic_slice_in_dim(w_mats[3:6], quarter * (own // 4), own // 4, 1)
    first = jnp.stack([to_chip(piece, count, s) for s in range(1, count // 2)])
    second = to_rep(first, rep_count, 1)
    rest = to_rep(jnp.stack([first, second]), rep_count, 2)
    pair = [to_pair(x, count) for x in (w_mats[3:6], first, second, rest)]
    return [w_mats, pair[0], first, second, rest] + pair[1:], quarter


def exchange_zero(y, count):
    out = []
    for shift in range(count // 2):
        held = y[2 * shift : 2 * shift + 2]
        if shift:
            held = to_chip(held, count, shift)
        out += [held[0], to_pair(held[1], count)]
    return out


def scatter_sum_zero(mine, away, count):
    held = mine.astype(f32) + to_pair(away, count).astype(f32)
    terms = [held[0]]
    for shift in range(1, count // 2):
        terms.append(to_chip(held[shift].astype(mine.dtype), count, shift).astype(f32))
    return terms


def sum_rep(x, count, dtype=f32):
    step = 1
    while step < count:
        low = x.astype(dtype)
        far = to_rep(low, count, step)
        x = low.astype(f32) + far.astype(f32)
        step *= 2
    return x


def dot(a, b, dims):
    return lax.dot_general(a, b, (dims, ((), ())), preferred_element_type=f32)


NN = ((1,), (0,))
NT = ((1,), (1,))
ANY = pl.BlockSpec(memory_space=pl.ANY)
VMEM_LIMIT = 60 * 1024 * 1024


def params(steps=1):
    return pltpu.CompilerParams(
        dimension_semantics=("arbitrary",) * steps, vmem_limit_bytes=VMEM_LIMIT
    )


def cost(flops, moved):
    return pl.CostEstimate(flops=int(flops), bytes_accessed=int(moved), transcendentals=0)


def project_body(index_ref, tok_a, tok_b, gain_ref, w_ref, scale_ref, *refs):
    normed_ref, qkv_ref, query_ref = refs[-3:]
    step = pl.program_id(0)
    tok = jnp.where(step == 0, tok_a[...], tok_b[...]).astype(f32)
    normed = (tok * rms_scale(tok) * gain_ref[...]).astype(bf16)
    normed_ref[0] = normed
    own = w_ref.shape[1]
    out = dot(w_ref[...].reshape(3 * own, -1), normed, NT)
    query = out[:own]
    query_ref[0] = query.astype(bf16)
    qkv_ref[0, :own] = (query * scale_ref[...]).astype(bf16)
    qkv_ref[0, own:] = out[own:].astype(bf16)


def project(owners, tok_a, tok_b, gain, w_mats, query_scale, count, held):
    rows, width = tok_a.shape
    own = w_mats.shape[1]
    shapes = (
        jax.ShapeDtypeStruct((count, rows, width), bf16),
        jax.ShapeDtypeStruct((count, 3 * own, rows), bf16),
        jax.ShapeDtypeStruct((count, own, rows), bf16),
    )
    whole = lambda *shape: pl.BlockSpec(shape, lambda s, at: (0,) * len(shape))
    held = () if held is None else tuple(held)
    return pl.pallas_call(
        project_body,
        out_shape=shapes,
        grid_spec=pltpu.PrefetchScalarGridSpec(
            num_scalar_prefetch=1,
            grid=(2,),
            in_specs=[
                whole(rows, width),
                whole(rows, width),
                whole(1, width),
                whole(3, own, width),
                whole(own, 1),
            ]
            + [ANY] * len(held),
            out_specs=[
                pl.BlockSpec((1, rows, width), lambda s, at: (at[s], 0, 0)),
                pl.BlockSpec((1, 3 * own, rows), lambda s, at: (at[s], 0, 0)),
                pl.BlockSpec((1, own, rows), lambda s, at: (at[s], 0, 0)),
            ],
        ),
        input_output_aliases={6 + i: i for i in range(len(held))},
        compiler_params=params(),
        cost_estimate=cost(2 * 2 * rows * 3 * own * width, 3 * own * width * 2 + 8 * rows * width),
        name="project",
    )(owners, tok_a, tok_b, gain, w_mats, query_scale, *held)


def masked_chunks(raw, size, diagonal, valid):
    chunks = []
    for j in range(raw.shape[0] // size):
        part = raw[j * size : (j + 1) * size]
        allowed = None
        if (j + 1) * size > PROMPT // 2:
            at = j * size + lax.broadcasted_iota(jnp.int32, part.shape, 0)
            allowed = at < valid
        if j == diagonal:
            causal = lax.broadcasted_iota(jnp.int32, part.shape, 0) <= lax.broadcasted_iota(
                jnp.int32, part.shape, 1
            )
            allowed = causal if allowed is None else allowed & causal
        chunks.append((part, allowed))
    return chunks


def units_of(count, prompt_rows, rows):
    for b in range(count):
        yield b, slice(0, prompt_rows), (b + 1) * prompt_rows, b, False
        yield b, slice(prompt_rows, rows), count * prompt_rows, None, True


def attend_body(valid_ref, place_ref, q_ref, k_ref, v_ref, att_ref, lse_ref, keys, values):
    count, _, rows = q_ref.shape
    size = PROMPT // count
    valid = valid_ref[0]
    for j in range(count):
        keys[j * size : (j + 1) * size, :] = k_ref[j, :, :size].T
        values[:, j * size : (j + 1) * size] = v_ref[j, :, :size]
    for b, lanes, seen, diagonal, own_cont in units_of(count, size, rows):
        query = q_ref[b, :, lanes]
        chunks = masked_chunks(dot(keys[:seen], query, NN), size, diagonal, valid)
        if own_cont:
            raw = dot(k_ref[b, :, size:].T, query, NN)
            chunks += masked_chunks(raw, raw.shape[0], 0, raw.shape[0])
        chunks = [p if ok is None else jnp.where(ok, p, NEG) for p, ok in chunks]
        top = chunks[0].max(axis=0, keepdims=True)
        for part in chunks[1:]:
            top = jnp.maximum(top, part.max(axis=0, keepdims=True))
        chunks = [jnp.exp(part - top) for part in chunks]
        total = chunks[0].sum(axis=0, keepdims=True)
        for part in chunks[1:]:
            total = total + part.sum(axis=0, keepdims=True)
        attended = None
        for j, part in enumerate(chunks):
            v_part = values[:, j * size : (j + 1) * size] if j * size < seen else v_ref[b, :, size:]
            term = dot(v_part, part.astype(bf16), NN)
            attended = term if attended is None else attended + term
        att_ref[place_ref[b], :, lanes] = (attended / total).astype(bf16)
        lse_ref[0, b : b + 1, lanes] = top + jnp.log(total)


def attend(valid, places, qkv, heads, head_dim):
    count, three_own, rows = qkv.shape
    own = three_own // 3
    block = lambda kind: pl.BlockSpec(
        (count, head_dim, rows), lambda h, *_: (0, kind * heads + h, 0)
    )
    pairs = PROMPT * PROMPT // 2 + PROMPT * count * (rows - PROMPT // count)
    return pl.pallas_call(
        attend_body,
        out_shape=(
            jax.ShapeDtypeStruct((count, own, rows), bf16),
            jax.ShapeDtypeStruct((heads, count, rows), f32),
        ),
        grid_spec=pltpu.PrefetchScalarGridSpec(
            num_scalar_prefetch=2,
            grid=(heads,),
            in_specs=[block(0), block(1), block(2)],
            out_specs=[
                pl.BlockSpec((count, head_dim, rows), lambda h, *_: (0, h, 0)),
                pl.BlockSpec((1, count, rows), lambda h, *_: (h, 0, 0)),
            ],
            scratch_shapes=[
                pltpu.VMEM((PROMPT, head_dim), bf16),
                pltpu.VMEM((head_dim, PROMPT), bf16),
            ],
        ),
        compiler_params=params(),
        cost_estimate=cost(4 * 256 * heads * pairs, qkv.size * 3),
        name="attend",
    )(valid, places, qkv, qkv, qkv)


def attend_back_body(
    valid_ref, place_ref, q_ref, k_ref, v_ref, query_ref, att_ref, lse_ref, scale_ref, *refs
):
    count, head_dim, rows = q_ref.shape
    parts = refs[:count]
    grad_ref, sum_ref, keys, values, grad_keys, grad_values, grad_att = refs[count:]
    size = PROMPT // count
    valid = valid_ref[0]
    for i in range(count):
        grad_att[place_ref[count + i]] = parts[i][...]
    for j in range(count):
        keys[j * size : (j + 1) * size, :] = k_ref[j, :, :size].T
        values[j * size : (j + 1) * size, :] = v_ref[j, :, :size].T
    grad_keys[...] = jnp.zeros_like(grad_keys)
    grad_values[...] = jnp.zeros_like(grad_values)
    scale_sum = jnp.zeros((head_dim, 1), f32)
    for b, lanes, seen, diagonal, own_cont in units_of(count, size, rows):
        query = q_ref[b, :, lanes]
        grad_out = grad_att[b, :, lanes]
        query_rows = query.T
        grad_rows = grad_out.T
        lse = lse_ref[0, b : b + 1, lanes]
        delta = jnp.sum(
            att_ref[place_ref[b], :, lanes].astype(f32) * grad_out.astype(f32),
            axis=0,
            keepdims=True,
        )
        grad_query = jnp.zeros(query.shape, f32)

        def block(key_rows, value_rows, chunk_size, diag, limit):
            raw = dot(key_rows, query, NN)
            grad_probs = dot(value_rows, grad_out, NN)
            probs, scores = [], []
            for j, (part, ok) in enumerate(masked_chunks(raw, chunk_size, diag, limit)):
                prob = jnp.exp(part - lse)
                if ok is not None:
                    prob = jnp.where(ok, prob, 0.0)
                score = prob * (grad_probs[j * chunk_size : (j + 1) * chunk_size] - delta)
                probs.append(prob.astype(bf16))
                scores.append(score.astype(bf16))
            return probs, scores

        probs, scores = block(keys[:seen], values[:seen], size, diagonal, valid)
        for j in range(len(probs)):
            at = slice(j * size, (j + 1) * size)
            grad_values[at, :] += dot(probs[j], grad_rows, NN)
            grad_keys[at, :] += dot(scores[j], query_rows, NN)
            grad_query += dot(k_ref[j, :, :size], scores[j], NN)
        if own_cont:
            probs, scores = block(
                k_ref[b, :, size:].T, v_ref[b, :, size:].T, rows - size, 0, rows - size
            )
            grad_query += dot(k_ref[b, :, size:], scores[0], NN)
            grad_ref[1, b, :, size:] = dot(scores[0], query_rows, NN).T.astype(bf16)
            grad_ref[2, b, :, size:] = dot(probs[0], grad_rows, NN).T.astype(bf16)
        scale_sum += jnp.sum(
            grad_query * query_ref[b, :, lanes].astype(f32), axis=1, keepdims=True
        )
        grad_ref[0, b, :, lanes] = (grad_query * scale_ref[:, 0:1]).astype(bf16)
    for j in range(count):
        at = slice(j * size, (j + 1) * size)
        grad_ref[1, j, :, :size] = grad_keys[at, :].T.astype(bf16)
        grad_ref[2, j, :, :size] = grad_values[at, :].T.astype(bf16)
    sum_ref[...] = jnp.broadcast_to(scale_sum, sum_ref.shape)


def attend_back(valid, places, qkv, query, att, lse, query_scale, parts, heads, head_dim):
    count, three_own, rows = qkv.shape
    own = three_own // 3
    size = PROMPT // count
    block = lambda kind: pl.BlockSpec(
        (count, head_dim, rows), lambda h, *_: (0, kind * heads + h, 0)
    )
    pairs = PROMPT * PROMPT // 2 + PROMPT * count * (rows - size)
    return pl.pallas_call(
        attend_back_body,
        out_shape=(
            jax.ShapeDtypeStruct((3, count, own, rows), bf16),
            jax.ShapeDtypeStruct((own, LANES), f32),
        ),
        grid_spec=pltpu.PrefetchScalarGridSpec(
            num_scalar_prefetch=2,
            grid=(heads,),
            in_specs=[
                block(0),
                block(1),
                block(2),
                block(0),
                block(0),
                pl.BlockSpec((1, count, rows), lambda h, *_: (h, 0, 0)),
                pl.BlockSpec((head_dim, 1), lambda h, *_: (h, 0)),
            ]
            + [pl.BlockSpec((head_dim, rows), lambda h, *_: (h, 0))] * count,
            out_specs=[
                pl.BlockSpec((3, count, head_dim, rows), lambda h, *_: (0, 0, h, 0)),
                pl.BlockSpec((head_dim, LANES), lambda h, *_: (h, 0)),
            ],
            scratch_shapes=[
                pltpu.VMEM((PROMPT, head_dim), bf16),
                pltpu.VMEM((PROMPT, head_dim), bf16),
                pltpu.VMEM((PROMPT, head_dim), f32),
                pltpu.VMEM((PROMPT, head_dim), f32),
                pltpu.VMEM((count, head_dim, rows), bf16),
            ],
        ),
        compiler_params=params(),
        cost_estimate=cost(10 * 256 * heads * pairs, qkv.size * 5),
        name="attend_back",
    )(valid, places, qkv, qkv, qkv, query, att, lse, query_scale, *parts)


def feed_body(place_ref, tok_ref, cot_ref, vec_ref, *refs):
    count = (place_ref.shape[0] - 1) // 2
    far = count // 2 - 1
    att_parts = refs[:count]
    w_own, w_pair, *w_far = refs[count : count + 8]
    (
        result_out,
        hidden_grad_out,
        att_grad_out,
        inputs_out,
        grads_out,
        sums_ref,
        w,
        att,
        hidden,
        weighted,
        inputs,
        grads,
        result,
        att_grad,
        att_sems,
        w_sems,
        out_sems,
    ) = refs[count + 8 :]
    rows, width = tok_ref.shape
    own = width // count
    quarter = own // 4
    tile = 2 * LANES
    tiles = width // tile

    def load(source, target, sem):
        one = pltpu.make_async_copy(source, target, sem)
        one.start()
        return one

    att_copies = [
        load(att_parts[i], att.at[place_ref[count + i]], att_sems.at[i]) for i in range(count)
    ]
    w_copies = []
    for m in range(3):
        group = []
        for flip in range(2):
            source = w_pair.at[m] if flip else w_own.at[3 + m]
            group.append(load(source, w.at[m, place_ref[count + flip]], w_sems.at[m, len(group)]))
            pieces = w_far[3 * flip : 3 * flip + 3]
            for s in range(far):
                at = place_ref[count + 2 * (s + 1) + flip]
                sources = [pieces[0].at[s], pieces[1].at[s], pieces[2].at[0, s], pieces[2].at[1, s]]
                for i in range(4):
                    start = pl.multiple_of((place_ref[2 * count] ^ i) * quarter, quarter)
                    target = w.at[m, at, pl.ds(start, quarter), :]
                    group.append(load(sources[i].at[m], target, w_sems.at[m, len(group)]))
        w_copies.append(group)
    stores = []

    def store(source, target):
        stores.append(load(source, target, out_sems.at[len(stores)]))

    def store_grads(m):
        for b in range(count):
            place = place_ref[b]
            at = (place % 2) * (far + 1) + place // 2
            store(grads.at[m, pl.ds(b * own, own), :], grads_out.at[m, at])

    grad_f = cot_ref[...]
    grads[2] = grad_f.T
    store_grads(2)
    for one in att_copies:
        one.wait()
    attended = att[...].reshape(width, rows).T
    inputs[0] = attended
    store(inputs.at[0], inputs_out.at[0])

    def w_rows(m, j):
        return w.at[m].reshape(width, width)[pl.ds(pl.multiple_of(j * tile, tile), tile), :]

    def w_cols(m, j):
        return w.at[m].reshape(width, width)[:, pl.ds(pl.multiple_of(j * tile, tile), tile)]

    def lanes(j):
        return pl.ds(pl.multiple_of(j * tile, tile), tile)

    for one in w_copies[0]:
        one.wait()

    def first(j, square):
        part = tok_ref[:, lanes(j)].astype(f32) + dot(attended, w_rows(0, j), NT)
        hidden[:, lanes(j)] = part
        return square + jnp.sum(part * part, axis=-1, keepdims=True)

    square = lax.fori_loop(0, tiles, first, jnp.zeros((rows, 1), f32))
    scale = lax.rsqrt(square / width + EPS)
    normed = (hidden[...] * scale * vec_ref[1:2, :]).astype(bf16)
    inputs[1] = normed
    store(inputs.at[1], inputs_out.at[1])
    for m in (1, 2):
        for one in w_copies[m]:
            one.wait()

    def second(j, carry):
        upper = dot(normed, w_rows(1, j), NT) + vec_ref[2:3, lanes(j)]
        gate = 1.0 / (1.0 + jnp.exp(-upper))
        inputs[2, :, lanes(j)] = (upper * gate).astype(bf16)
        grad_act = dot(grad_f, w_cols(2, j), NN)
        grad_up = (grad_act * gate * (1.0 + upper * (1.0 - gate))).astype(bf16)
        result[:, lanes(j)] = grad_up
        sums_ref[1:2, lanes(j)] = jnp.sum(grad_up.astype(f32), axis=0, keepdims=True)
        sums_ref[2:3, lanes(j)] = jnp.sum(
            cot_ref[:, lanes(j)].astype(f32), axis=0, keepdims=True
        )
        return carry

    lax.fori_loop(0, tiles, second, 0)
    store(inputs.at[2], inputs_out.at[2])
    grad_up = result[...]
    grads[1] = grad_up.T
    store_grads(1)
    activ = inputs[2]

    def third(j, inner):
        part = hidden[:, lanes(j)]
        out = dot(activ, w_rows(2, j), NT) + vec_ref[3:4, lanes(j)]
        result[:, lanes(j)] = (part + out).astype(bf16)
        grad_normed = dot(grad_up, w_cols(1, j), NN)
        sums_ref[0:1, lanes(j)] = jnp.sum(grad_normed * part * scale, axis=0, keepdims=True)
        turn = grad_normed * vec_ref[1:2, lanes(j)]
        weighted[:, lanes(j)] = turn
        return inner + jnp.sum(part * turn, axis=-1, keepdims=True)

    inner = lax.fori_loop(0, tiles, third, jnp.zeros((rows, 1), f32)) / width
    store(result, result_out)
    back = cot_ref[...].astype(f32) + (
        scale * weighted[...] - hidden[...] * (scale * scale * scale) * inner
    )
    weighted[...] = back
    store(weighted, hidden_grad_out)
    branch = back.astype(bf16)

    def fourth(j, carry):
        att_grad[lanes(j), :] = dot(branch, w_cols(0, j), NN).astype(bf16).T
        return carry

    lax.fori_loop(0, tiles, fourth, 0)
    for b in range(count):
        store(att_grad.at[pl.ds(b * own, own), :], att_grad_out.at[place_ref[b]])
    grads[0] = branch.T
    store_grads(0)
    for one in stores:
        one.wait()


def feed(places, tokens, cotangent, vec, att_parts, w_parts):
    count = len(att_parts)
    rows, width = tokens.shape
    own = width // count
    whole = lambda *shape: pl.BlockSpec(shape, lambda i, at: (0,) * len(shape))
    return pl.pallas_call(
        feed_body,
        out_shape=(
            jax.ShapeDtypeStruct((rows, width), bf16),
            jax.ShapeDtypeStruct((rows, width), f32),
            jax.ShapeDtypeStruct((count, own, rows), bf16),
            jax.ShapeDtypeStruct((3, rows, width), bf16),
            jax.ShapeDtypeStruct((3, count, own, rows), bf16),
            jax.ShapeDtypeStruct((8, width), f32),
        ),
        grid_spec=pltpu.PrefetchScalarGridSpec(
            num_scalar_prefetch=1,
            grid=(1,),
            in_specs=[whole(rows, width), whole(rows, width), whole(*vec.shape)]
            + [ANY] * (count + len(w_parts)),
            out_specs=[ANY] * 5 + [whole(8, width)],
            scratch_shapes=[
                pltpu.VMEM((3, count, own, width), bf16),
                pltpu.VMEM((count, own, rows), bf16),
                pltpu.VMEM((rows, width), f32),
                pltpu.VMEM((rows, width), f32),
                pltpu.VMEM((3, rows, width), bf16),
                pltpu.VMEM((3, width, rows), bf16),
                pltpu.VMEM((rows, width), bf16),
                pltpu.VMEM((width, rows), bf16),
                pltpu.SemaphoreType.DMA((count,)),
                pltpu.SemaphoreType.DMA((3, 2 + 8 * (count // 2 - 1))),
                pltpu.SemaphoreType.DMA((5 + 4 * count,)),
            ],
        ),
        compiler_params=params(),
        cost_estimate=cost(12 * rows * width * width, 3 * width * width * 2 + rows * width * 24),
        name="feed",
    )(places, tokens, cotangent, vec, *att_parts, *w_parts)


def outer_body(grad_ref, input_ref, mine_ref, away_ref):
    count = grad_ref.shape[1]
    chips = count // 2
    for b in range(count):
        out = dot(grad_ref[0, b], input_ref[0], NN).astype(bf16)
        if b < chips:
            mine_ref[b, 0] = out
        else:
            away_ref[b - chips, 0] = out


def outer(grads, inputs):
    mats, count, own, rows = grads.shape
    width = count * own
    half = jax.ShapeDtypeStruct((count // 2, mats, own, width), bf16)
    half_spec = pl.BlockSpec((count // 2, 1, own, width), lambda m: (0, m, 0, 0))
    return pl.pallas_call(
        outer_body,
        out_shape=(half, half),
        grid=(mats,),
        in_specs=[
            pl.BlockSpec((1, count, own, rows), lambda m: (m, 0, 0, 0)),
            pl.BlockSpec((1, rows, width), lambda m: (m, 0, 0)),
        ],
        out_specs=[half_spec, half_spec],
        compiler_params=params(),
        cost_estimate=cost(2 * mats * width * width * rows, mats * width * (width + rows) * 4),
        name="outer",
    )(grads, inputs)


def ortho_body(left_ref, out_ref):
    rank = left_ref.shape[0]
    columns = [left_ref[c] for c in range(rank)]
    for e in range(rank):
        done = columns[e]
        done = done * lax.rsqrt(jnp.sum(done * done, axis=-1, keepdims=True) + EPS)
        out_ref[e] = done
        for c in range(e + 1, rank):
            columns[c] = columns[c] - jnp.sum(done * columns[c], axis=-1, keepdims=True) * done


def orthonormal(left):
    return pl.pallas_call(
        ortho_body, out_shape=jax.ShapeDtypeStruct(left.shape, f32), name="ortho"
    )(left)


def on_device(
    tokens,
    cotangent,
    weights,
    vectors,
    error,
    previous_right_factors,
    momentum,
    vec_momentum,
    prompt_len,
):
    zero_index = lax.axis_index("zero")
    rep_index = lax.axis_index("rep")
    n = lax.axis_size("zero")
    rep_count = lax.axis_size("rep")
    rows, width = tokens.shape
    head_dim = width // HEADS
    heads = HEADS // n
    own = weights.shape[0]
    group_rows = n * rows
    sources, receivers, places = relative(zero_index, n)
    maps = jnp.concatenate([places, sources])
    w_mats = weights.transpose(1, 0, 2)

    tok_parts = gather_zero(tokens, n)
    vec_parts = gather_zero(vectors, n)
    full_v = jnp.zeros((n,) + vectors.shape, bf16)
    for i in range(n):
        full_v = lax.dynamic_update_slice(full_v, vec_parts[i][None], (sources[i], 0, 0))
    vec_float = full_v.transpose(1, 0, 2).reshape(-1, width).astype(f32)
    far_parts, quarter = gather_weights(w_mats, n, rep_index, rep_count)
    feed_maps = jnp.concatenate([maps, quarter[None]])

    scale_raw = vectors[4].astype(f32)
    scale_const = LOG2E / math.sqrt(head_dim)
    query_scale = (scale_const * jax.nn.softplus(scale_raw)).reshape(own, 1)
    held = None
    for s in range(n // 2):
        held = project(
            sources[2 * s : 2 * s + 2],
            tok_parts[2 * s],
            tok_parts[2 * s + 1],
            vec_float[0:1],
            w_mats,
            query_scale,
            n,
            held,
        )
    normed_all, qkv, query = held
    att_heads, lse = attend(prompt_len, places, qkv, heads, head_dim)
    att_parts = exchange_zero(att_heads, n)
    result, grad_hidden, att_grad, far_inputs, far_grads, sums = feed(
        feed_maps, tokens, cotangent, vec_float, att_parts, far_parts
    )
    grad_parts = exchange_zero(att_grad, n)
    mine, away = outer(far_grads, far_inputs)
    paired = to_pair(away, n)
    far_sums = [(mine[s] + paired[s].astype(f32)).astype(bf16) for s in range(1, n // 2)]
    grad_parts, far_sums = lax.optimization_barrier((grad_parts, far_sums))
    far_terms = [mine[0].astype(f32), paired[0].astype(f32)]
    for s in range(1, n // 2):
        far_terms.append(to_chip(far_sums[s - 1], n, s).astype(f32))

    grads, scale_sums = attend_back(
        prompt_len, maps, qkv, query, att_heads, lse, query_scale, grad_parts, heads, head_dim
    )
    near_block = jnp.einsum("mbot,bti->moi", grads, normed_all, preferred_element_type=f32)
    grad_n1_part = jnp.einsum(
        "mbot,moi->bti", grads, w_mats[0:3], preferred_element_type=f32
    ).astype(bf16)
    part_of = lambda at: lax.dynamic_index_in_dim(grad_n1_part, at, 0, keepdims=False)
    n1_terms = scatter_sum_zero(
        jnp.stack([part_of(receivers[i]) for i in range(0, n, 2)]),
        jnp.stack([part_of(receivers[i]) for i in range(1, n, 2)]),
        n,
    )
    grad_n1 = sum(n1_terms[1:], n1_terms[0])
    tok_float = tokens.astype(f32)
    scale_one = rms_scale(tok_float)
    gain_one = vec_float[0]
    grad_tokens = grad_hidden + norm_back(tok_float, scale_one, gain_one, grad_n1)

    grad_scale_raw = scale_sums[:, 0] * scale_const * jax.nn.sigmoid(scale_raw)
    vec_terms = jnp.concatenate(
        [jnp.sum(grad_n1 * tok_float * scale_one, axis=0)[None], sums[0:3]], axis=0
    )
    vec_blocks = vec_terms.reshape(4, n, own).transpose(1, 0, 2)
    vec_of = lambda at: lax.dynamic_index_in_dim(vec_blocks, at, 0, keepdims=False)
    vec_block = sum(
        scatter_sum_zero(
            jnp.stack([vec_of(receivers[i]) for i in range(0, n, 2)]),
            jnp.stack([vec_of(receivers[i]) for i in range(1, n, 2)]),
            n,
        )
    )
    vec_total = sum_rep(jnp.concatenate([vec_block, grad_scale_raw[None]], axis=0), rep_count)

    far_block = sum(far_terms[1:], far_terms[0])
    merged = jnp.concatenate([near_block, far_block], axis=0) + error.transpose(1, 0, 2)
    old_right = previous_right_factors.transpose(0, 2, 1)
    left = jnp.einsum("moi,mri->rmo", merged, old_right, precision=PRECISION_HIGH)
    ortho = orthonormal(sum_rep(left, rep_count) / rep_count)
    right = jnp.einsum("moi,rmo->mri", merged, ortho, precision=PRECISION_HIGH)
    right = sum_rep(right, rep_count, bf16) / rep_count
    fresh_right_factors = right.transpose(0, 2, 1)
    approximation = jnp.einsum("rmo,mri->moi", ortho, right, precision=PRECISION_HIGH)
    new_error = (merged - approximation).transpose(1, 0, 2)

    rep_width = width // rep_count
    own_right = lax.dynamic_slice_in_dim(right, rep_index * rep_width, rep_width, 2)
    own_grads = jnp.einsum("mri,rmo->mio", own_right, ortho, precision=PRECISION_HIGH)
    step_rate = 0.03 / math.sqrt(group_rows)
    own_momentum = MU * momentum.transpose(1, 2, 0) + own_grads
    grad_weights = own_grads.transpose(2, 0, 1)
    new_momentum = own_momentum.transpose(2, 0, 1)
    update_weights = (-step_rate * own_momentum).transpose(2, 0, 1)
    grad_vectors = vec_total / rep_count
    new_vec_momentum = MU * vec_momentum + grad_vectors
    update_vectors = -step_rate * new_vec_momentum
    return (
        result,
        grad_tokens,
        grad_weights,
        grad_vectors,
        new_error,
        fresh_right_factors,
        new_momentum,
        new_vec_momentum,
        update_weights,
        update_vectors,
    )


def solution(mesh):
    in_specs = (
        P(("rep", "zero"), None),
        P(("rep", "zero"), None),
        P("zero", None, None),
        P(None, "zero"),
        P(("rep", "zero"), None, None),
        P(None, None, "zero"),
        P("zero", None, "rep"),
        P(None, "zero"),
        P("rep"),
    )
    out_specs = (
        P(("rep", "zero"), None),
        P(("rep", "zero"), None),
        P("zero", None, "rep"),
        P(None, "zero"),
        P(("rep", "zero"), None, None),
        P(None, None, "zero"),
        P("zero", None, "rep"),
        P(None, "zero"),
        P("zero", None, "rep"),
        P(None, "zero"),
    )

    return jax.shard_map(
        on_device, mesh=mesh, in_specs=in_specs, out_specs=out_specs, check_vma=False
    )
```

```python
import functools
import math

import jax
import jax.numpy as jnp
import numpy as np
from jax import lax
from jax.experimental import pallas as pl
from jax.experimental.pallas import tpu as pltpu
from jax.sharding import PartitionSpec as P


HEADS = 16
PROMPT = 1024
LANES = 128

EPS = 1e-06
MU = 0.9
LOG2E = 1.442695041
NEG = -1e30
f32 = jnp.float32
bf16 = jnp.bfloat16


def rms_scale(field):
    return lax.rsqrt(jnp.mean(field * field, axis=-1, keepdims=True) + EPS)


def norm_back(field, scale, gain_vec, grad_in):
    weighted = grad_in * gain_vec
    inner = jnp.mean(field * weighted, axis=-1, keepdims=True)
    return scale * weighted - field * (scale * scale * scale) * inner


def to_pair(x, count):
    return lax.ppermute(x, "zero", [(i, i ^ 1) for i in range(count)])


def to_chip(x, count, shift):
    return lax.ppermute(x, "zero", [(i, (i + 2 * shift) % count) for i in range(count)])


def to_rep(x, count, step):
    return lax.ppermute(x, "rep", [(i, i ^ step) for i in range(count)])


def tables(chip, core, chips, quarter):
    at = np.arange(2 * chips)
    sign = np.repeat([-1, -1, 1], 2 * chips)
    shift = np.concatenate([at // 2, -(at // 2), at % chips])
    sign[2 * chips : 4 * chips] = 1
    flip = np.concatenate([at % 2, at % 2, at // chips])
    sign, shift, flip = (np.append(a, 0).astype(np.int32) for a in (sign, shift, flip))
    found = lax.rem(sign * chip + shift + chips, jnp.int32(chips)) * 2 + (core ^ flip)
    return jnp.where(np.arange(6 * chips + 1) == 6 * chips, quarter, found).astype(jnp.int32)


def gather_zero(x, count):
    out = []
    for shift in range(count // 2):
        block = x if shift == 0 else to_chip(x, count, shift)
        out += [block, to_pair(block, count)]
    return out


def sum_zero(x, count):
    x = x + to_pair(x, count)
    return sum((to_chip(x, count, s) for s in range(1, count // 2)), x)


def gather_weights(w_mats, count, quarter, rep_count):
    own = w_mats.shape[1]
    start = (3, quarter * (own // 4), 0)
    piece = lax.dynamic_slice(w_mats, start, (3, own // 4, w_mats.shape[2]))
    first = jnp.stack([to_chip(piece, count, s) for s in range(1, count // 2)])
    second = to_rep(first, rep_count, 1)
    third = to_rep(first, rep_count, 2)
    fourth = to_rep(second, rep_count, 2)
    mine = w_mats[3:6]
    far = [first, second, third, fourth]
    return [w_mats, to_pair(mine, count)] + far + [to_pair(x, count) for x in far]


def exchange_zero(near, far, count):
    out = [near[0], to_pair(near[1], count)]
    for shift in range(1, count // 2):
        held = to_chip(far[shift - 1], count, shift)
        out += [held, to_pair(held[1], count)]
    return out


def scatter_sum_zero(mine, away, count):
    held = mine.astype(f32) + to_pair(away, count).astype(f32)
    terms = [held[0]]
    for shift in range(1, count // 2):
        terms.append(to_chip(held[shift].astype(mine.dtype), count, shift).astype(f32))
    return terms


def sum_rep(x, count, dtype=f32):
    step = 1
    while step < count:
        low = x.astype(dtype)
        x = low.astype(f32) + to_rep(low, count, step).astype(f32)
        step *= 2
    return x


def dot(a, b, dims):
    return lax.dot_general(a, b, (dims, ((), ())), preferred_element_type=f32)


NN = ((1,), (0,))
NT = ((1,), (1,))
TN = ((0,), (0,))
ANY = pl.BlockSpec(memory_space=pl.ANY)
VMEM_LIMIT = 60 * 1024 * 1024


def params(steps=1):
    return pltpu.CompilerParams(
        dimension_semantics=("arbitrary",) * steps, vmem_limit_bytes=VMEM_LIMIT
    )


def cost(flops, moved):
    return pl.CostEstimate(flops=int(flops), bytes_accessed=int(moved), transcendentals=0)


def project_body(index_ref, tok_a, tok_b, gain_ref, w_ref, scale_ref, *refs):
    normed_ref, qkv_ref, query_ref = refs[-3:]
    step = pl.program_id(0)
    tok = jnp.where(step == 0, tok_a[...], tok_b[...]).astype(f32)
    normed = (tok * rms_scale(tok) * gain_ref[...]).astype(bf16)
    normed_ref[0] = normed
    own = w_ref.shape[1]
    out = dot(w_ref[...].reshape(3 * own, -1), normed, NT)
    query = out[:own]
    query_ref[0] = query.astype(bf16)
    qkv_ref[0, :own] = (query * scale_ref[...]).astype(bf16)
    qkv_ref[0, own:] = out[own:].astype(bf16)


def project(maps, shift, tok_a, tok_b, gain, w_mats, query_scale, count, held):
    first = count + 2 * shift
    rows, width = tok_a.shape
    own = w_mats.shape[1]
    shapes = (
        jax.ShapeDtypeStruct((count, rows, width), bf16),
        jax.ShapeDtypeStruct((count, 3 * own, rows), bf16),
        jax.ShapeDtypeStruct((count, own, rows), bf16),
    )
    whole = lambda *shape: pl.BlockSpec(shape, lambda s, at: (0,) * len(shape))
    held = () if held is None else tuple(held)
    return pl.pallas_call(
        project_body,
        out_shape=shapes,
        grid_spec=pltpu.PrefetchScalarGridSpec(
            num_scalar_prefetch=1,
            grid=(2,),
            in_specs=[
                whole(rows, width),
                whole(rows, width),
                whole(1, width),
                whole(3, own, width),
                whole(own, 1),
            ]
            + [ANY] * len(held),
            out_specs=[
                pl.BlockSpec((1, rows, width), lambda s, at: (at[first + s], 0, 0)),
                pl.BlockSpec((1, 3 * own, rows), lambda s, at: (at[first + s], 0, 0)),
                pl.BlockSpec((1, own, rows), lambda s, at: (at[first + s], 0, 0)),
            ],
        ),
        input_output_aliases={6 + i: i for i in range(len(held))},
        compiler_params=params(),
        cost_estimate=cost(2 * 2 * rows * 3 * own * width, 3 * own * width * 2 + 8 * rows * width),
    )(maps, tok_a, tok_b, gain, w_mats, query_scale, *held)


def masked_chunks(raw, size, diagonal, valid):
    chunks = []
    for j in range(raw.shape[0] // size):
        part = raw[j * size : (j + 1) * size]
        allowed = None
        if (j + 1) * size > PROMPT // 2:
            at = j * size + lax.broadcasted_iota(jnp.int32, part.shape, 0)
            allowed = at < valid
        if j == diagonal:
            causal = lax.broadcasted_iota(jnp.int32, part.shape, 0) <= lax.broadcasted_iota(
                jnp.int32, part.shape, 1
            )
            allowed = causal if allowed is None else allowed & causal
        chunks.append((part, allowed))
    return chunks


def units_of(count, prompt_rows, rows):
    for b in range(count):
        yield b, slice(0, prompt_rows), (b + 1) * prompt_rows, b, False
        yield b, slice(prompt_rows, rows), count * prompt_rows, None, True


def attend_body(valid_ref, place_ref, q_ref, k_ref, v_ref, *refs):
    count, _, rows = q_ref.shape
    *outs, all_ref, lse_ref, keys, values = refs
    size = PROMPT // count
    valid = valid_ref[0]
    for j in range(count):
        keys[j * size : (j + 1) * size, :] = k_ref[j, :, :size].T
        values[:, j * size : (j + 1) * size] = v_ref[j, :, :size]
    for b, lanes, seen, diagonal, own_cont in units_of(count, size, rows):
        query = q_ref[b, :, lanes]
        chunks = masked_chunks(dot(keys[:seen], query, NN), size, diagonal, valid)
        if own_cont:
            raw = dot(k_ref[b, :, size:].T, query, NN)
            chunks += masked_chunks(raw, raw.shape[0], 0, raw.shape[0])
        chunks = [p if ok is None else jnp.where(ok, p, NEG) for p, ok in chunks]
        top = chunks[0].max(axis=0, keepdims=True)
        for part in chunks[1:]:
            top = jnp.maximum(top, part.max(axis=0, keepdims=True))
        chunks = [jnp.exp(part - top) for part in chunks]
        total = chunks[0].sum(axis=0, keepdims=True)
        for part in chunks[1:]:
            total = total + part.sum(axis=0, keepdims=True)
        attended = None
        for j, part in enumerate(chunks):
            v_part = values[:, j * size : (j + 1) * size] if j * size < seen else v_ref[b, :, size:]
            term = dot(v_part, part.astype(bf16), NN)
            attended = term if attended is None else attended + term
        all_ref[b, :, lanes] = (attended / total).astype(bf16)
        lse_ref[0, b : b + 1, lanes] = top + jnp.log(total)
    chips = count // 2
    for p in range(count):
        block = all_ref[place_ref[2 * count + (p % 2) * chips + p // 2]]
        if p < 2:
            outs[p][...] = block
        else:
            outs[p // 2 + 1][p % 2] = block


def attend(valid, places, qkv, heads, head_dim):
    count, three_own, rows = qkv.shape
    own = three_own // 3
    block = lambda kind: pl.BlockSpec(
        (count, head_dim, rows), lambda h, *_: (0, kind * heads + h, 0)
    )
    pairs = PROMPT * PROMPT // 2 + PROMPT * count * (rows - PROMPT // count)
    return pl.pallas_call(
        attend_body,
        out_shape=(
            *[jax.ShapeDtypeStruct((own, rows), bf16)] * 2,
            *[jax.ShapeDtypeStruct((2, own, rows), bf16)] * (count // 2 - 1),
            jax.ShapeDtypeStruct((count, own, rows), bf16),
            jax.ShapeDtypeStruct((heads, count, rows), f32),
        ),
        grid_spec=pltpu.PrefetchScalarGridSpec(
            num_scalar_prefetch=2,
            grid=(heads,),
            in_specs=[block(0), block(1), block(2)],
            out_specs=[pl.BlockSpec((head_dim, rows), lambda h, *_: (h, 0))] * 2
            + [pl.BlockSpec((2, head_dim, rows), lambda h, *_: (0, h, 0))] * (count // 2 - 1)
            + [
                pl.BlockSpec((count, head_dim, rows), lambda h, *_: (0, h, 0)),
                pl.BlockSpec((1, count, rows), lambda h, *_: (h, 0, 0)),
            ],
            scratch_shapes=[
                pltpu.VMEM((PROMPT, head_dim), bf16),
                pltpu.VMEM((head_dim, PROMPT), bf16),
            ],
        ),
        compiler_params=params(),
        cost_estimate=cost(4 * 256 * heads * pairs, qkv.size * 3),
    )(valid, places, qkv, qkv, qkv)


def attend_back_body(
    valid_ref, place_ref, q_ref, k_ref, v_ref, query_ref, att_ref, lse_ref, scale_ref, spread_ref, *refs
):
    count, head_dim, rows = q_ref.shape
    parts = refs[:count]
    grad_ref, sum_ref, left_ref, keys, values, grad_keys, grad_values, grad_att = refs[count:]
    size = PROMPT // count
    valid = valid_ref[0]
    for i in range(count):
        grad_att[place_ref[count + i]] = parts[i][...].reshape(head_dim, rows)
    for j in range(count):
        keys[j * size : (j + 1) * size, :] = k_ref[j, :, :size].T
        values[j * size : (j + 1) * size, :] = v_ref[j, :, :size].T
    grad_keys[...] = jnp.zeros_like(grad_keys)
    grad_values[...] = jnp.zeros_like(grad_values)
    scale_sum = jnp.zeros((head_dim, 1), f32)
    for b, lanes, seen, diagonal, own_cont in units_of(count, size, rows):
        query = q_ref[b, :, lanes]
        grad_out = grad_att[b, :, lanes]
        query_rows = query.T
        grad_rows = grad_out.T
        lse = lse_ref[0, b : b + 1, lanes]
        delta = jnp.sum(
            att_ref[b, :, lanes].astype(f32) * grad_out.astype(f32),
            axis=0,
            keepdims=True,
        )
        grad_query = jnp.zeros(query.shape, f32)

        def block(key_rows, value_rows, chunk_size, diag, limit):
            raw = dot(key_rows, query, NN)
            grad_probs = dot(value_rows, grad_out, NN)
            probs, scores = [], []
            for j, (part, ok) in enumerate(masked_chunks(raw, chunk_size, diag, limit)):
                prob = jnp.exp(part - lse)
                if ok is not None:
                    prob = jnp.where(ok, prob, 0.0)
                score = prob * (grad_probs[j * chunk_size : (j + 1) * chunk_size] - delta)
                probs.append(prob.astype(bf16))
                scores.append(score.astype(bf16))
            return probs, scores

        probs, scores = block(keys[:seen], values[:seen], size, diagonal, valid)
        for j in range(len(probs)):
            at = slice(j * size, (j + 1) * size)
            grad_values[at, :] += dot(probs[j], grad_rows, NN)
            grad_keys[at, :] += dot(scores[j], query_rows, NN)
            grad_query += dot(k_ref[j, :, :size], scores[j], NN)
        if own_cont:
            probs, scores = block(
                k_ref[b, :, size:].T, v_ref[b, :, size:].T, rows - size, 0, rows - size
            )
            grad_query += dot(k_ref[b, :, size:], scores[0], NN)
            grad_ref[1, b, :, size:] = dot(scores[0], query_rows, NN).T.astype(bf16)
            grad_ref[2, b, :, size:] = dot(probs[0], grad_rows, NN).T.astype(bf16)
        scale_sum += jnp.sum(
            grad_query * query_ref[b, :, lanes].astype(f32), axis=1, keepdims=True
        )
        grad_ref[0, b, :, lanes] = (grad_query * scale_ref[:, 0:1]).astype(bf16)
    for j in range(count):
        at = slice(j * size, (j + 1) * size)
        grad_ref[1, j, :, :size] = grad_keys[at, :].T.astype(bf16)
        grad_ref[2, j, :, :size] = grad_values[at, :].T.astype(bf16)
    sum_ref[...] = jnp.broadcast_to(scale_sum, sum_ref.shape)
    twice = spread_ref.shape[1] // 3
    for m in range(3):
        left = jnp.zeros((twice, head_dim), f32)
        for b in range(count):
            terms = spread_ref[b, m * twice : (m + 1) * twice]
            left += dot(terms, grad_ref[m, b], NT)
        left_ref[0, m, :, :head_dim] = left[: twice // 2] + left[twice // 2 :]


def attend_back(valid, places, qkv, query, att, lse, query_scale, terms, parts, heads, head_dim):
    count, three_own, rows = qkv.shape
    own = three_own // 3
    size = PROMPT // count
    block = lambda kind: pl.BlockSpec(
        (count, head_dim, rows), lambda h, *_: (0, kind * heads + h, 0)
    )
    pairs = PROMPT * PROMPT // 2 + PROMPT * count * (rows - size)
    return pl.pallas_call(
        attend_back_body,
        out_shape=(
            jax.ShapeDtypeStruct((3, count, own, rows), bf16),
            jax.ShapeDtypeStruct((own, LANES), f32),
            jax.ShapeDtypeStruct((heads, 3, terms.shape[1] // 6, LANES), f32),
        ),
        grid_spec=pltpu.PrefetchScalarGridSpec(
            num_scalar_prefetch=2,
            grid=(heads,),
            in_specs=[
                block(0),
                block(1),
                block(2),
                block(0),
                block(0),
                pl.BlockSpec((1, count, rows), lambda h, *_: (h, 0, 0)),
                pl.BlockSpec((head_dim, 1), lambda h, *_: (h, 0)),
                pl.BlockSpec(terms.shape, lambda h, *_: (0, 0, 0)),
            ]
            + [
                pl.BlockSpec((1, head_dim, rows), lambda h, *_: (0, h, 0))
                if part.ndim == 3
                else pl.BlockSpec((head_dim, rows), lambda h, *_: (h, 0))
                for part in parts
            ],
            out_specs=[
                pl.BlockSpec((3, count, head_dim, rows), lambda h, *_: (0, 0, h, 0)),
                pl.BlockSpec((head_dim, LANES), lambda h, *_: (h, 0)),
                pl.BlockSpec((1, 3, terms.shape[1] // 6, LANES), lambda h, *_: (h, 0, 0, 0)),
            ],
            scratch_shapes=[
                pltpu.VMEM((PROMPT, head_dim), bf16),
                pltpu.VMEM((PROMPT, head_dim), bf16),
                pltpu.VMEM((PROMPT, head_dim), f32),
                pltpu.VMEM((PROMPT, head_dim), f32),
                pltpu.VMEM((count, head_dim, rows), bf16),
            ],
        ),
        compiler_params=params(),
        cost_estimate=cost(10 * 256 * heads * pairs, qkv.size * 5),
    )(valid, places, qkv, qkv, qkv, query, att, lse, query_scale, terms, *parts)


def feed_body(place_ref, tok_ref, cot_ref, vec_ref, *refs):
    count = (place_ref.shape[0] - 1) // 3
    far = count // 2 - 1
    att_parts = refs[:count]
    w_own, w_pair, *w_far = refs[count : count + 10]
    outs = refs[count + 10 :]
    att_grad_outs, outs = outs[: far + 2], outs[far + 2 :]
    (
        result_out,
        hidden_grad_out,
        inputs_out,
        grads_out,
        sums_ref,
        w,
        att,
        hidden,
        weighted,
        inputs,
        grads,
        result,
        att_grad,
        att_sems,
        w_sems,
        out_sems,
    ) = outs
    rows, width = tok_ref.shape
    own = width // count
    quarter = own // 4
    tile = 2 * LANES
    tiles = width // tile

    def load(source, target, sem):
        one = pltpu.make_async_copy(source, target, sem)
        one.start()
        return one

    att_copies = [
        load(
            att_parts[i].at[0] if i > 1 and i % 2 == 0 else att_parts[i],
            att.at[place_ref[count + i]],
            att_sems.at[i],
        )
        for i in range(count)
    ]
    w_copies = []
    for m in range(3):
        group = []
        for flip in range(2):
            source = w_pair.at[m] if flip else w_own.at[3 + m]
            group.append(load(source, w.at[m, place_ref[count + flip]], w_sems.at[m, len(group)]))
            pieces = w_far[4 * flip : 4 * flip + 4]
            for s in range(far):
                at = place_ref[count + 2 * (s + 1) + flip]
                for i in range(4):
                    start = pl.multiple_of((place_ref[3 * count] ^ i) * quarter, quarter)
                    target = w.at[m, at, pl.ds(start, quarter), :]
                    group.append(load(pieces[i].at[s, m], target, w_sems.at[m, len(group)]))
        w_copies.append(group)
    stores = []

    def store(source, target):
        stores.append(load(source, target, out_sems.at[len(stores)]))

    def rows_of(ref, p):
        return ref.at[pl.ds(pl.multiple_of(place_ref[2 * count + p] * own, own), own), :]

    def store_grads(m):
        for p in range(count):
            store(rows_of(grads.at[m], p), grads_out.at[m, p])

    grad_f = cot_ref[...]
    grads[2] = grad_f.T
    store_grads(2)
    for one in att_copies:
        one.wait()
    attended = att[...].reshape(width, rows).T
    inputs[0] = attended
    store(inputs.at[0], inputs_out.at[0])

    def w_rows(m, j):
        return w.at[m].reshape(width, width)[pl.ds(pl.multiple_of(j * tile, tile), tile), :]

    def w_cols(m, j):
        return w.at[m].reshape(width, width)[:, pl.ds(pl.multiple_of(j * tile, tile), tile)]

    def lanes(j):
        return pl.ds(pl.multiple_of(j * tile, tile), tile)

    for one in w_copies[0]:
        one.wait()

    def first(j, square):
        part = tok_ref[:, lanes(j)].astype(f32) + dot(attended, w_rows(0, j), NT)
        hidden[:, lanes(j)] = part
        return square + jnp.sum(part * part, axis=-1, keepdims=True)

    square = lax.fori_loop(0, tiles, first, jnp.zeros((rows, 1), f32))
    scale = lax.rsqrt(square / width + EPS)
    normed = (hidden[...] * scale * vec_ref[1:2, :]).astype(bf16)
    inputs[1] = normed
    store(inputs.at[1], inputs_out.at[1])
    for m in (1, 2):
        for one in w_copies[m]:
            one.wait()

    def second(j, carry):
        upper = dot(normed, w_rows(1, j), NT) + vec_ref[2:3, lanes(j)]
        gate = 1.0 / (1.0 + jnp.exp(-upper))
        inputs[2, :, lanes(j)] = (upper * gate).astype(bf16)
        grad_act = dot(grad_f, w_cols(2, j), NN)
        grad_up = (grad_act * gate * (1.0 + upper * (1.0 - gate))).astype(bf16)
        result[:, lanes(j)] = grad_up
        sums_ref[1:2, lanes(j)] = jnp.sum(grad_up.astype(f32), axis=0, keepdims=True)
        sums_ref[2:3, lanes(j)] = jnp.sum(
            cot_ref[:, lanes(j)].astype(f32), axis=0, keepdims=True
        )
        return carry

    lax.fori_loop(0, tiles, second, 0)
    store(inputs.at[2], inputs_out.at[2])
    grad_up = result[...]
    grads[1] = grad_up.T
    store_grads(1)
    activ = inputs[2]

    def third(j, inner):
        part = hidden[:, lanes(j)]
        out = dot(activ, w_rows(2, j), NT) + vec_ref[3:4, lanes(j)]
        result[:, lanes(j)] = (part + out).astype(bf16)
        grad_normed = dot(grad_up, w_cols(1, j), NN)
        sums_ref[0:1, lanes(j)] = jnp.sum(grad_normed * part * scale, axis=0, keepdims=True)
        turn = grad_normed * vec_ref[1:2, lanes(j)]
        weighted[:, lanes(j)] = turn
        return inner + jnp.sum(part * turn, axis=-1, keepdims=True)

    inner = lax.fori_loop(0, tiles, third, jnp.zeros((rows, 1), f32)) / width
    store(result, result_out)
    back = cot_ref[...].astype(f32) + (
        scale * weighted[...] - hidden[...] * (scale * scale * scale) * inner
    )
    weighted[...] = back
    store(weighted, hidden_grad_out)
    branch = back.astype(bf16)

    def fourth(j, carry):
        att_grad[lanes(j), :] = dot(branch, w_cols(0, j), NN).astype(bf16).T
        return carry

    lax.fori_loop(0, tiles, fourth, 0)
    for p in range(count):
        target = att_grad_outs[p] if p < 2 else att_grad_outs[p // 2 + 1].at[p % 2]
        store(rows_of(att_grad, (p % 2) * (far + 1) + p // 2), target)
    grads[0] = branch.T
    store_grads(0)
    for one in stores:
        one.wait()


def feed(places, tokens, cotangent, vec, att_parts, w_parts):
    count = len(att_parts)
    rows, width = tokens.shape
    own = width // count
    whole = lambda *shape: pl.BlockSpec(shape, lambda i, at: (0,) * len(shape))
    return pl.pallas_call(
        feed_body,
        out_shape=(
            *[jax.ShapeDtypeStruct((own, rows), bf16)] * 2,
            *[jax.ShapeDtypeStruct((2, own, rows), bf16)] * (count // 2 - 1),
            jax.ShapeDtypeStruct((rows, width), bf16),
            jax.ShapeDtypeStruct((rows, width), f32),
            jax.ShapeDtypeStruct((3, rows, width), bf16),
            jax.ShapeDtypeStruct((3, count, own, rows), bf16),
            jax.ShapeDtypeStruct((8, width), f32),
        ),
        grid_spec=pltpu.PrefetchScalarGridSpec(
            num_scalar_prefetch=1,
            grid=(1,),
            in_specs=[whole(rows, width), whole(rows, width), whole(*vec.shape)]
            + [ANY] * (count + len(w_parts)),
            out_specs=[ANY] * (5 + count // 2) + [whole(8, width)],
            scratch_shapes=[
                pltpu.VMEM((3, count, own, width), bf16),
                pltpu.VMEM((count, own, rows), bf16),
                pltpu.VMEM((rows, width), f32),
                pltpu.VMEM((rows, width), f32),
                pltpu.VMEM((3, rows, width), bf16),
                pltpu.VMEM((3, width, rows), bf16),
                pltpu.VMEM((rows, width), bf16),
                pltpu.VMEM((width, rows), bf16),
                pltpu.SemaphoreType.DMA((count,)),
                pltpu.SemaphoreType.DMA((3, 2 + 8 * (count // 2 - 1))),
                pltpu.SemaphoreType.DMA((5 + 4 * count,)),
            ],
        ),
        compiler_params=params(),
        cost_estimate=cost(12 * rows * width * width, 3 * width * width * 2 + rows * width * 24),
    )(places, tokens, cotangent, vec, *att_parts, *w_parts)


def split(x):
    high = x.astype(bf16)
    return jnp.concatenate([high, (x - high.astype(f32)).astype(bf16)], axis=-2)


def fold(x, rank):
    return x[..., :rank, :] + x[..., rank:, :]


def outer_body(grad_ref, input_ref, right_ref, *refs):
    *outs, left_mine_ref, left_away_ref = refs
    count, own, rows = grad_ref.shape[1:]
    chips = count // 2
    twice = right_ref.shape[1]
    grads = grad_ref[0]
    out = dot(grads.reshape(count * own, rows), input_ref[0], NN).astype(bf16)
    for b in range(count):
        outs[b][0] = out[b * own : (b + 1) * own]
    spread = dot(right_ref[...].reshape(count * twice, -1), input_ref[0], NT)
    for b in range(count):
        terms = split(fold(spread[b * twice : (b + 1) * twice], twice // 2))
        left = fold(dot(terms, grads[b], NT), twice // 2)
        if b < chips:
            left_mine_ref[b, 0] = left
        else:
            left_away_ref[b - chips, 0] = left


def outer(grads, inputs, rights):
    mats, count, own, rows = grads.shape
    width = count * own
    twice = rights.shape[1] // mats
    chips = count // 2
    left = jax.ShapeDtypeStruct((chips, mats, twice // 2, own), f32)
    part = jax.ShapeDtypeStruct((mats, own, width), bf16)
    part_spec = pl.BlockSpec((1, own, width), lambda m: (m, 0, 0))
    left_spec = pl.BlockSpec((chips, 1, twice // 2, own), lambda m: (0, m, 0, 0))
    return pl.pallas_call(
        outer_body,
        out_shape=(*[part] * count, left, left),
        grid=(mats,),
        in_specs=[
            pl.BlockSpec((1, count, own, rows), lambda m: (m, 0, 0, 0)),
            pl.BlockSpec((1, rows, width), lambda m: (m, 0, 0)),
            pl.BlockSpec((count, twice, width), lambda m: (0, m, 0)),
        ],
        out_specs=[part_spec] * count + [left_spec] * 2,
        compiler_params=params(),
        cost_estimate=cost(2 * mats * width * width * rows, mats * width * (width + rows) * 4),
    )(grads, inputs, rights)


def spread_body(normed_ref, right_ref, out_ref):
    mats_twice = right_ref.shape[0]
    twice = mats_twice // 3
    out = dot(right_ref[...], normed_ref[0], NT)
    for m in range(3):
        at = slice(m * twice, (m + 1) * twice)
        out_ref[0, at] = split(fold(out[at], twice // 2))


def spread(normed, rights):
    count, rows, width = normed.shape
    size = rights.shape[0]
    return pl.pallas_call(
        spread_body,
        out_shape=jax.ShapeDtypeStruct((count, size, rows), bf16),
        grid=(count,),
        in_specs=[
            pl.BlockSpec((1, rows, width), lambda b: (b, 0, 0)),
            pl.BlockSpec((size, width), lambda b: (0, 0)),
        ],
        out_specs=pl.BlockSpec((1, size, rows), lambda b: (b, 0, 0)),
        compiler_params=params(),
        cost_estimate=cost(2 * count * rows * width * size, normed.size * 2),
    )(normed, rights)


def error_left_body(error_ref, right_ref, out_ref):
    rank = right_ref.shape[1]
    error = error_ref[0]
    high = error.astype(bf16)
    low = (error - high.astype(f32)).astype(bf16)
    rights = split(right_ref[0])
    out = dot(high, rights, NT) + dot(low, rights, NT)
    out_ref[0] = fold(out.T, rank)


def error_left(error, right):
    mats, own, width = error.shape
    rank = right.shape[1]
    return pl.pallas_call(
        error_left_body,
        out_shape=jax.ShapeDtypeStruct((mats, rank, own), f32),
        grid=(mats,),
        in_specs=[
            pl.BlockSpec((1, own, width), lambda m: (m, 0, 0)),
            pl.BlockSpec((1, rank, width), lambda m: (m, 0, 0)),
        ],
        out_specs=pl.BlockSpec((1, rank, own), lambda m: (m, 0, 0)),
        compiler_params=params(),
        cost_estimate=cost(4 * error.size * rank, error.size * 4),
    )(error, right)


def input_back_body(order_ref, grad_ref, w_ref, *refs):
    count = len(refs) - 2
    tok_refs = refs[:count]
    out_ref, sum_ref = refs[count:]
    step = pl.program_id(0)
    own, rows = grad_ref.shape[2:]
    grads = grad_ref[...].reshape(3 * own, rows)
    part = dot(grads, w_ref[...].reshape(3 * own, -1), TN)
    out_ref[0] = part.astype(bf16)
    tok = tok_refs[0][...]
    for i in range(1, count):
        tok = jnp.where(step == i, tok_refs[i][...], tok)
    tok = tok.astype(f32)
    total = jnp.sum(part * (tok * rms_scale(tok)), axis=0, keepdims=True)

    @pl.when(step == 0)
    def _():
        sum_ref[...] = jnp.zeros_like(sum_ref)

    sum_ref[...] += jnp.broadcast_to(total, sum_ref.shape)


def input_back(maps, flip, grads, w_mats, toks):
    _, total, own, rows = grads.shape
    count = total // 2
    first = 2 * total + flip * count
    width = w_mats.shape[-1]
    return pl.pallas_call(
        input_back_body,
        out_shape=(
            jax.ShapeDtypeStruct((count, rows, width), bf16),
            jax.ShapeDtypeStruct((8, width), f32),
        ),
        grid_spec=pltpu.PrefetchScalarGridSpec(
            num_scalar_prefetch=1,
            grid=(count,),
            in_specs=[
                pl.BlockSpec((3, 1, own, rows), lambda s, at: (0, at[first + s], 0, 0)),
                pl.BlockSpec((3, own, width), lambda s, at: (0, 0, 0)),
            ]
            + [pl.BlockSpec((rows, width), lambda s, at: (0, 0))] * count,
            out_specs=[
                pl.BlockSpec((1, rows, width), lambda s, at: (s, 0, 0)),
                pl.BlockSpec((8, width), lambda s, at: (0, 0)),
            ],
        ),
        compiler_params=params(),
        cost_estimate=cost(2 * grads.size * width, grads.size * 2 + count * rows * width * 4),
    )(maps, grads, w_mats, *toks)


def right_body(ortho_ref, *refs):
    *terms, out = refs
    merged = sum(term[0].astype(f32) for term in terms)
    rank = ortho_ref.shape[1]
    out[0] = fold(dot(split(ortho_ref[0]), merged.astype(bf16), NN), rank).astype(bf16)


def tile_specs(rows, tile, first):
    return (
        pl.BlockSpec((1, rows, tile), lambda m, j: (first + m, 0, j)),
        pl.BlockSpec((1, rows, tile), lambda m, j: (m, 0, j)),
    )


def right_factors(ortho, error, first, terms):
    mats, own, width = terms[0].shape
    rank = ortho.shape[1]
    tile = width
    error_spec, term_spec = tile_specs(own, tile, first)
    return pl.pallas_call(
        right_body,
        out_shape=jax.ShapeDtypeStruct((mats, rank, width), bf16),
        grid=(mats, width // tile),
        in_specs=[pl.BlockSpec((1, rank, own), lambda m, j: (first + m, 0, 0)), error_spec]
        + [term_spec] * len(terms),
        out_specs=tile_specs(rank, tile, first)[1],
        compiler_params=params(2),
        cost_estimate=cost(4 * mats * own * width * rank, mats * own * width * 6),
    )(ortho, error, *terms)


def triple(x, pattern):
    high = x.astype(bf16)
    low = (x - high.astype(f32)).astype(bf16)
    return jnp.concatenate([low if p else high for p in pattern], axis=0)


def finish_body(rate, count, ortho_ref, right_ref, slice_ref, mom_ref, *refs):
    terms = refs[:count]
    err_ref, fresh_ref, grad_ref, new_ref, upd_ref = refs[-5:]
    ortho = triple(ortho_ref[0], (0, 0, 1))
    fresh_ref[0] = right_ref[0]
    approx = dot(ortho, triple(right_ref[0], (0, 1, 0)), TN)
    err_ref[0] = sum(term[0].astype(f32) for term in terms) - approx

    @pl.when(pl.program_id(1) == 0)
    def _():
        grad = dot(triple(slice_ref[0], (0, 1, 0)), ortho, TN)
        grad_ref[0] = grad
        new = MU * mom_ref[0] + grad
        new_ref[0] = new
        upd_ref[0] = -rate * new


def finish(rate, ortho, right, right_slice, momentum, error, first, terms, held):
    half, own, width = terms[0].shape
    mats, rank = ortho.shape[:2]
    cut = momentum.shape[1]
    tile = width
    error_spec, term_spec = tile_specs(own, tile, first)
    fresh_spec, right_spec = tile_specs(rank, tile, first)
    per = lambda *shape: pl.BlockSpec((1,) + shape, lambda m, j: (m, 0, 0))
    at = lambda *shape: pl.BlockSpec((1,) + shape, lambda m, j: (first + m, 0, 0))
    shape = jax.ShapeDtypeStruct(momentum.shape, f32)
    held = () if held is None else tuple(held)
    return pl.pallas_call(
        functools.partial(finish_body, rate, 1 + len(terms)),
        out_shape=(
            jax.ShapeDtypeStruct((mats, own, width), f32),
            jax.ShapeDtypeStruct((mats, rank, width), f32),
            shape,
            shape,
            shape,
        ),
        grid=(half, width // tile),
        in_specs=[at(rank, own), right_spec, per(rank, cut), at(cut, own), error_spec]
        + [term_spec] * len(terms)
        + [ANY] * len(held),
        out_specs=[error_spec, fresh_spec] + [at(cut, own)] * 3,
        input_output_aliases={5 + len(terms) + i: i for i in range(len(held))},
        compiler_params=params(2),
        cost_estimate=cost(half * own * width * 48, half * own * width * 10),
    )(ortho, right, right_slice, momentum, error, *terms, *held)


def close_rows_body(tok_ref, gain_ref, hidden_ref, mine_ref, paired_ref, *refs):
    *far, out = refs
    grad = mine_ref[0].astype(f32) + paired_ref[0].astype(f32)
    for term in far:
        grad += term[...].astype(f32)
    tok = tok_ref[...].astype(f32)
    out[...] = hidden_ref[...] + norm_back(tok, rms_scale(tok), gain_ref[...], grad)


def close_rows(tokens, gain, grad_hidden, mine, paired, far):
    rows, width = tokens.shape
    row = pl.BlockSpec((LANES, width), lambda i: (i, 0))
    first = pl.BlockSpec((1, LANES, width), lambda i: (0, i, 0))
    return pl.pallas_call(
        close_rows_body,
        out_shape=jax.ShapeDtypeStruct((rows, width), f32),
        grid=(rows // LANES,),
        in_specs=[row, pl.BlockSpec((1, width), lambda i: (0, 0)), row, first, first]
        + [row] * len(far),
        out_specs=row,
        compiler_params=params(),
        cost_estimate=cost(20 * rows * width, 18 * rows * width),
    )(tokens, gain, grad_hidden, mine, paired, *far)


def ortho_body(left_ref, out_ref):
    rank = left_ref.shape[0]
    columns = [left_ref[c] for c in range(rank)]
    for e in range(rank):
        done = columns[e]
        done = done * lax.rsqrt(jnp.sum(done * done, axis=-1, keepdims=True) + EPS)
        out_ref[:, e, :] = done
        for c in range(e + 1, rank):
            columns[c] = columns[c] - jnp.sum(done * columns[c], axis=-1, keepdims=True) * done


def orthonormal(left):
    rank, mats, own = left.shape
    return pl.pallas_call(
        ortho_body, out_shape=jax.ShapeDtypeStruct((mats, rank, own), f32)
    )(left)


def on_device(
    tokens,
    cotangent,
    weights,
    vectors,
    error,
    previous_right_factors,
    momentum,
    vec_momentum,
    prompt_len,
):
    zero_index = lax.axis_index("zero")
    rep_index = lax.axis_index("rep")
    n = lax.axis_size("zero")
    chips = n // 2
    rep_count = lax.axis_size("rep")
    rows, width = tokens.shape
    head_dim = width // HEADS
    heads = HEADS // n
    own = weights.shape[0]
    group_rows = n * rows
    quarter = rep_index & 3
    maps = tables(zero_index >> 1, zero_index & 1, chips, quarter)
    w_mats = weights.transpose(1, 0, 2)
    old_right = previous_right_factors.transpose(0, 2, 1)
    rank = old_right.shape[1]
    error_mats = error.transpose(1, 0, 2)

    column = zero_index * own
    spaced = lax.dynamic_update_slice(jnp.zeros((5, width), bf16), vectors, (0, column))
    spaced = sum((to_chip(spaced, n, s) for s in range(1, chips)), spaced)
    vec_float = (spaced + to_pair(spaced, n)).astype(f32)
    tok_parts = gather_zero(tokens, n)
    pairs_right = split(old_right)
    right_parts = gather_zero(pairs_right[3:6].reshape(6 * rank, width), n)
    flipped = [2 * ((chips - s) % chips) + f for f in range(2) for s in range(chips)]
    far_rights = jnp.stack([right_parts[i] for i in flipped])
    error_part = error_left(error_mats, old_right)
    far_parts = gather_weights(w_mats, n, quarter, rep_count)

    scale_raw = vectors[4].astype(f32)
    scale_const = LOG2E / math.sqrt(head_dim)
    query_scale = (scale_const * jax.nn.softplus(scale_raw)).reshape(own, 1)
    held = None
    for s in range(chips):
        held = project(
            maps,
            s,
            tok_parts[2 * s],
            tok_parts[2 * s + 1],
            vec_float[0:1],
            w_mats,
            query_scale,
            n,
            held,
        )
    normed_all, qkv, query = held
    *att_blocks, att_all, lse = attend(prompt_len, maps, qkv, heads, head_dim)
    att_parts = exchange_zero(att_blocks[:2], att_blocks[2:], n)
    terms = spread(normed_all, pairs_right[0:3].reshape(6 * rank, width))
    *att_grads, result, grad_hidden, far_inputs, far_grads, sums = feed(
        maps, tokens, cotangent, vec_float, att_parts, far_parts
    )
    grad_parts = exchange_zero(att_grads[:2], att_grads[2:], n)
    *blocks, left_mine, left_away = outer(far_grads, far_inputs, far_rights)
    far_sums = []
    for s in range(1, chips):
        paired = to_pair(blocks[chips + s], n)
        far_sums.append((blocks[s].astype(f32) + paired.astype(f32)).astype(bf16))
    left_far = sum(scatter_sum_zero(left_mine, left_away, n))
    grad_parts, far_sums = lax.optimization_barrier((grad_parts, far_sums))
    far_terms = [to_chip(far_sums[s - 1], n, s) for s in range(1, chips)]
    grads, scale_sums, left_heads = attend_back(
        prompt_len,
        maps,
        qkv,
        query,
        att_all,
        lse,
        query_scale,
        terms,
        grad_parts,
        heads,
        head_dim,
    )
    left_near = left_heads[..., :head_dim].transpose(1, 2, 0, 3).reshape(3, rank, own)
    left = jnp.concatenate([left_near, left_far], axis=0) + error_part
    left = sum_rep(left.transpose(1, 0, 2), rep_count) / rep_count
    ortho = orthonormal(left)

    toks = [tok_parts[i] for i in flipped]
    n1_away, gain_away = input_back(maps, 1, grads, w_mats, toks[chips:])
    n1_mine, gain_mine = input_back(maps, 0, grads, w_mats, toks[:chips])
    near = jnp.einsum("mbot,bti->moi", grads, normed_all, preferred_element_type=f32)
    n1_paired = to_pair(n1_away, n)
    n1_far = []
    for s in range(1, chips):
        sent = (n1_mine[s].astype(f32) + n1_paired[s].astype(f32)).astype(bf16)
        n1_far.append(to_chip(sent, n, s))
    grad_tokens = close_rows(tokens, vec_float[0:1], grad_hidden, n1_mine, n1_paired, n1_far)

    near_terms = [near]
    far_terms = [blocks[0], to_pair(blocks[chips], n), *far_terms]
    rep_width = width // rep_count
    cut_at = rep_index * rep_width
    step_rate = 0.03 / math.sqrt(group_rows)
    momentum_mats = momentum.transpose(1, 2, 0)

    def close(right, cut_at, first, parts, held):
        own_right = lax.dynamic_slice_in_dim(right, cut_at, rep_width, 1)
        right, own_right = (x[: 3 * rank].reshape(3, rank, -1) for x in (right, own_right))
        return finish(
            step_rate, ortho, right, own_right, momentum_mats, error_mats, first, parts, held
        )

    right = right_factors(ortho, error_mats, 0, near_terms).reshape(3 * rank, width)
    right = sum_rep(right, rep_count, bf16) / rep_count
    held = close(right, cut_at, 0, near_terms, None)

    vec_sums = jnp.concatenate([gain_away[0:1] + gain_mine[0:1], sums[0:3]], axis=0)
    vec_sums = lax.dynamic_slice_in_dim(sum_zero(vec_sums, n), column, own, 1)
    grad_scale_raw = scale_sums[:, 0] * scale_const * jax.nn.sigmoid(scale_raw)
    vec_sums = jnp.concatenate([vec_sums, grad_scale_raw[None]], axis=0)
    vec_rows = -(-vec_sums.size // width)
    vec_flat = jnp.pad(vec_sums.reshape(-1), (0, vec_rows * width - vec_sums.size))
    vec_flat = vec_flat.reshape(vec_rows, width).astype(bf16)
    right = right_factors(ortho, error_mats, 3, far_terms)
    packed = jnp.concatenate([right.reshape(3 * rank, width), vec_flat], axis=0)
    packed = sum_rep(packed, rep_count, bf16) / rep_count
    held = close(packed, lax.optimization_barrier(cut_at), 3, far_terms, held)
    new_error, fresh, *moved = held
    new_error = new_error.transpose(1, 0, 2)
    fresh_right_factors = fresh.transpose(0, 2, 1)
    grad_weights, new_momentum, update_weights = (x.transpose(2, 0, 1) for x in moved)
    grad_vectors = packed[3 * rank :].reshape(-1)[: vec_sums.size].reshape(vec_sums.shape)
    new_vec_momentum = MU * vec_momentum + grad_vectors
    update_vectors = -step_rate * new_vec_momentum
    return (
        result,
        grad_tokens,
        grad_weights,
        grad_vectors,
        new_error,
        fresh_right_factors,
        new_momentum,
        new_vec_momentum,
        update_weights,
        update_vectors,
    )


def solution(mesh):
    in_specs = (
        P(("rep", "zero"), None),
        P(("rep", "zero"), None),
        P("zero", None, None),
        P(None, "zero"),
        P(("rep", "zero"), None, None),
        P(None, None, "zero"),
        P("zero", None, "rep"),
        P(None, "zero"),
        P("rep"),
    )
    out_specs = (
        P(("rep", "zero"), None),
        P(("rep", "zero"), None),
        P("zero", None, "rep"),
        P(None, "zero"),
        P(("rep", "zero"), None, None),
        P(None, None, "zero"),
        P("zero", None, "rep"),
        P(None, "zero"),
        P("zero", None, "rep"),
        P(None, "zero"),
    )

    return jax.shard_map(
        on_device, mesh=mesh, in_specs=in_specs, out_specs=out_specs, check_vma=False
    )
```

```python
import functools
import math

import jax
import jax.numpy as jnp
import numpy as np
from jax import lax
from jax.experimental import pallas as pl
from jax.experimental.pallas import tpu as pltpu
from jax.sharding import PartitionSpec as P


HEADS = 16
PROMPT = 1024
LANES = 128

EPS = 1e-06
MU = 0.9
LOG2E = 1.442695041
NEG = -1e30
f32 = jnp.float32
bf16 = jnp.bfloat16


def rms_scale(field):
    return lax.rsqrt(jnp.mean(field * field, axis=-1, keepdims=True) + EPS)


def norm_back(field, scale, gain_vec, grad_in):
    weighted = grad_in * gain_vec
    inner = jnp.mean(field * weighted, axis=-1, keepdims=True)
    return scale * weighted - field * (scale * scale * scale) * inner


def to_pair(x, count):
    return lax.ppermute(x, "zero", [(i, i ^ 1) for i in range(count)])


def to_chip(x, count, shift):
    return lax.ppermute(x, "zero", [(i, (i + 2 * shift) % count) for i in range(count)])


def to_rep(x, count, step):
    return lax.ppermute(x, "rep", [(i, i ^ step) for i in range(count)])


def tables(chip, core, chips, quarter):
    at = np.arange(2 * chips)
    sign = np.repeat([-1, -1, 1], 2 * chips)
    shift = np.concatenate([at // 2, -(at // 2), at % chips])
    sign[2 * chips : 4 * chips] = 1
    flip = np.concatenate([at % 2, at % 2, at // chips])
    sign, shift, flip = (np.append(a, 0).astype(np.int32) for a in (sign, shift, flip))
    found = lax.rem(sign * chip + shift + chips, jnp.int32(chips)) * 2 + (core ^ flip)
    return jnp.where(np.arange(6 * chips + 1) == 6 * chips, quarter, found).astype(jnp.int32)


def gather_zero(x, count):
    out = []
    for shift in range(count // 2):
        block = x if shift == 0 else to_chip(x, count, shift)
        out += [block, to_pair(block, count)]
    return out


def sum_zero(x, count):
    x = x + to_pair(x, count)
    return sum((to_chip(x, count, s) for s in range(1, count // 2)), x)


def gather_weights(w_mats, count, quarter, rep_count):
    own = w_mats.shape[1]
    start = (3, quarter * (own // 4), 0)
    piece = lax.dynamic_slice(w_mats, start, (3, own // 4, w_mats.shape[2]))
    first = jnp.stack([to_chip(piece, count, s) for s in range(1, count // 2)])
    second = to_rep(first, rep_count, 1)
    third = to_rep(first, rep_count, 2)
    fourth = to_rep(second, rep_count, 2)
    mine = w_mats[3:6]
    far = [first, second, third, fourth]
    return [w_mats, to_pair(mine, count)] + far + [to_pair(x, count) for x in far]


def exchange_zero(near, far, count):
    out = [near[0], to_pair(near[1], count)]
    for shift in range(1, count // 2):
        held = to_chip(far[shift - 1], count, shift)
        out += [held, to_pair(held[1], count)]
    return out


def scatter_sum_zero(mine, away, count):
    held = mine.astype(f32) + to_pair(away, count).astype(f32)
    terms = [held[0]]
    for shift in range(1, count // 2):
        terms.append(to_chip(held[shift].astype(mine.dtype), count, shift).astype(f32))
    return terms


def sum_rep(x, count, dtype=f32):
    step = 1
    while step < count:
        low = x.astype(dtype)
        x = low.astype(f32) + to_rep(low, count, step).astype(f32)
        step *= 2
    return x


def dot(a, b, dims):
    return lax.dot_general(a, b, (dims, ((), ())), preferred_element_type=f32)


NN = ((1,), (0,))
NT = ((1,), (1,))
TN = ((0,), (0,))
ANY = pl.BlockSpec(memory_space=pl.ANY)
VMEM_LIMIT = 60 * 1024 * 1024


def params(steps=1):
    return pltpu.CompilerParams(
        dimension_semantics=("arbitrary",) * steps, vmem_limit_bytes=VMEM_LIMIT
    )


def cost(flops, moved):
    return pl.CostEstimate(flops=int(flops), bytes_accessed=int(moved), transcendentals=0)


def project_body(index_ref, tok_a, tok_b, gain_ref, w_ref, scale_ref, *refs):
    normed_ref, qkv_ref, query_ref = refs[-3:]
    step = pl.program_id(0)
    tok = jnp.where(step == 0, tok_a[...], tok_b[...]).astype(f32)
    normed = (tok * rms_scale(tok) * gain_ref[...]).astype(bf16)
    normed_ref[0] = normed
    own = w_ref.shape[1]
    out = dot(w_ref[...].reshape(3 * own, -1), normed, NT)
    query = out[:own]
    query_ref[0] = query.astype(bf16)
    qkv_ref[0, :own] = (query * scale_ref[...]).astype(bf16)
    qkv_ref[0, own:] = out[own:].astype(bf16)


def project(maps, shift, tok_a, tok_b, gain, w_mats, query_scale, count, held):
    first = count + 2 * shift
    rows, width = tok_a.shape
    own = w_mats.shape[1]
    shapes = (
        jax.ShapeDtypeStruct((count, rows, width), bf16),
        jax.ShapeDtypeStruct((count, 3 * own, rows), bf16),
        jax.ShapeDtypeStruct((count, own, rows), bf16),
    )
    whole = lambda *shape: pl.BlockSpec(shape, lambda s, at: (0,) * len(shape))
    held = () if held is None else tuple(held)
    return pl.pallas_call(
        project_body,
        out_shape=shapes,
        grid_spec=pltpu.PrefetchScalarGridSpec(
            num_scalar_prefetch=1,
            grid=(2,),
            in_specs=[
                whole(rows, width),
                whole(rows, width),
                whole(1, width),
                whole(3, own, width),
                whole(own, 1),
            ]
            + [ANY] * len(held),
            out_specs=[
                pl.BlockSpec((1, rows, width), lambda s, at: (at[first + s], 0, 0)),
                pl.BlockSpec((1, 3 * own, rows), lambda s, at: (at[first + s], 0, 0)),
                pl.BlockSpec((1, own, rows), lambda s, at: (at[first + s], 0, 0)),
            ],
        ),
        input_output_aliases={6 + i: i for i in range(len(held))},
        compiler_params=params(),
        cost_estimate=cost(2 * 2 * rows * 3 * own * width, 3 * own * width * 2 + 8 * rows * width),
    )(maps, tok_a, tok_b, gain, w_mats, query_scale, *held)


def masked_chunks(raw, size, diagonal, valid):
    chunks = []
    for j in range(raw.shape[0] // size):
        part = raw[j * size : (j + 1) * size]
        allowed = None
        if (j + 1) * size > PROMPT // 2:
            at = j * size + lax.broadcasted_iota(jnp.int32, part.shape, 0)
            allowed = at < valid
        if j == diagonal:
            causal = lax.broadcasted_iota(jnp.int32, part.shape, 0) <= lax.broadcasted_iota(
                jnp.int32, part.shape, 1
            )
            allowed = causal if allowed is None else allowed & causal
        chunks.append((part, allowed))
    return chunks


def units_of(count, prompt_rows, rows):
    for b in range(count):
        yield b, slice(0, prompt_rows), (b + 1) * prompt_rows, b, False
        yield b, slice(prompt_rows, rows), count * prompt_rows, None, True


def attend_body(valid_ref, place_ref, q_ref, k_ref, v_ref, *refs):
    count, _, rows = q_ref.shape
    *outs, all_ref, lse_ref, keys, values = refs
    size = PROMPT // count
    valid = valid_ref[0]
    for j in range(count):
        keys[j * size : (j + 1) * size, :] = k_ref[j, :, :size].T
        values[:, j * size : (j + 1) * size] = v_ref[j, :, :size]
    for b, lanes, seen, diagonal, own_cont in units_of(count, size, rows):
        query = q_ref[b, :, lanes]
        chunks = masked_chunks(dot(keys[:seen], query, NN), size, diagonal, valid)
        if own_cont:
            raw = dot(k_ref[b, :, size:].T, query, NN)
            chunks += masked_chunks(raw, raw.shape[0], 0, raw.shape[0])
        chunks = [p if ok is None else jnp.where(ok, p, NEG) for p, ok in chunks]
        top = chunks[0].max(axis=0, keepdims=True)
        for part in chunks[1:]:
            top = jnp.maximum(top, part.max(axis=0, keepdims=True))
        chunks = [jnp.exp(part - top) for part in chunks]
        total = chunks[0].sum(axis=0, keepdims=True)
        for part in chunks[1:]:
            total = total + part.sum(axis=0, keepdims=True)
        attended = None
        for j, part in enumerate(chunks):
            v_part = values[:, j * size : (j + 1) * size] if j * size < seen else v_ref[b, :, size:]
            term = dot(v_part, part.astype(bf16), NN)
            attended = term if attended is None else attended + term
        all_ref[b, :, lanes] = (attended / total).astype(bf16)
        lse_ref[0, b : b + 1, lanes] = top + jnp.log(total)
    chips = count // 2
    for p in range(count):
        block = all_ref[place_ref[2 * count + (p % 2) * chips + p // 2]]
        if p < 2:
            outs[p][...] = block
        else:
            outs[p // 2 + 1][p % 2] = block


def attend(valid, places, qkv, heads, head_dim):
    count, three_own, rows = qkv.shape
    own = three_own // 3
    block = lambda kind: pl.BlockSpec(
        (count, head_dim, rows), lambda h, *_: (0, kind * heads + h, 0)
    )
    pairs = PROMPT * PROMPT // 2 + PROMPT * count * (rows - PROMPT // count)
    return pl.pallas_call(
        attend_body,
        out_shape=(
            *[jax.ShapeDtypeStruct((own, rows), bf16)] * 2,
            *[jax.ShapeDtypeStruct((2, own, rows), bf16)] * (count // 2 - 1),
            jax.ShapeDtypeStruct((count, own, rows), bf16),
            jax.ShapeDtypeStruct((heads, count, rows), f32),
        ),
        grid_spec=pltpu.PrefetchScalarGridSpec(
            num_scalar_prefetch=2,
            grid=(heads,),
            in_specs=[block(0), block(1), block(2)],
            out_specs=[pl.BlockSpec((head_dim, rows), lambda h, *_: (h, 0))] * 2
            + [pl.BlockSpec((2, head_dim, rows), lambda h, *_: (0, h, 0))] * (count // 2 - 1)
            + [
                pl.BlockSpec((count, head_dim, rows), lambda h, *_: (0, h, 0)),
                pl.BlockSpec((1, count, rows), lambda h, *_: (h, 0, 0)),
            ],
            scratch_shapes=[
                pltpu.VMEM((PROMPT, head_dim), bf16),
                pltpu.VMEM((head_dim, PROMPT), bf16),
            ],
        ),
        compiler_params=params(),
        cost_estimate=cost(4 * 256 * heads * pairs, qkv.size * 3),
    )(valid, places, qkv, qkv, qkv)


def attend_back_body(
    valid_ref, place_ref, q_ref, k_ref, v_ref, query_ref, att_ref, lse_ref, scale_ref, spread_ref, *refs
):
    count, head_dim, rows = q_ref.shape
    parts = refs[:count]
    grad_ref, sum_ref, left_ref, keys, values, grad_keys, grad_values, grad_att = refs[count:]
    size = PROMPT // count
    valid = valid_ref[0]
    for i in range(count):
        grad_att[place_ref[count + i]] = parts[i][...].reshape(head_dim, rows)
    for j in range(count):
        keys[j * size : (j + 1) * size, :] = k_ref[j, :, :size].T
        values[j * size : (j + 1) * size, :] = v_ref[j, :, :size].T
    grad_keys[...] = jnp.zeros_like(grad_keys)
    grad_values[...] = jnp.zeros_like(grad_values)
    scale_sum = jnp.zeros((head_dim, 1), f32)
    for b, lanes, seen, diagonal, own_cont in units_of(count, size, rows):
        query = q_ref[b, :, lanes]
        grad_out = grad_att[b, :, lanes]
        query_rows = query.T
        grad_rows = grad_out.T
        lse = lse_ref[0, b : b + 1, lanes]
        delta = jnp.sum(
            att_ref[b, :, lanes].astype(f32) * grad_out.astype(f32),
            axis=0,
            keepdims=True,
        )
        grad_query = jnp.zeros(query.shape, f32)

        def block(key_rows, value_rows, chunk_size, diag, limit):
            raw = dot(key_rows, query, NN)
            grad_probs = dot(value_rows, grad_out, NN)
            probs, scores = [], []
            for j, (part, ok) in enumerate(masked_chunks(raw, chunk_size, diag, limit)):
                prob = jnp.exp(part - lse)
                if ok is not None:
                    prob = jnp.where(ok, prob, 0.0)
                score = prob * (grad_probs[j * chunk_size : (j + 1) * chunk_size] - delta)
                probs.append(prob.astype(bf16))
                scores.append(score.astype(bf16))
            return probs, scores

        probs, scores = block(keys[:seen], values[:seen], size, diagonal, valid)
        for j in range(len(probs)):
            at = slice(j * size, (j + 1) * size)
            grad_values[at, :] += dot(probs[j], grad_rows, NN)
            grad_keys[at, :] += dot(scores[j], query_rows, NN)
            grad_query += dot(k_ref[j, :, :size], scores[j], NN)
        if own_cont:
            probs, scores = block(
                k_ref[b, :, size:].T, v_ref[b, :, size:].T, rows - size, 0, rows - size
            )
            grad_query += dot(k_ref[b, :, size:], scores[0], NN)
            grad_ref[1, b, :, size:] = dot(scores[0], query_rows, NN).T.astype(bf16)
            grad_ref[2, b, :, size:] = dot(probs[0], grad_rows, NN).T.astype(bf16)
        scale_sum += jnp.sum(
            grad_query * query_ref[b, :, lanes].astype(f32), axis=1, keepdims=True
        )
        grad_ref[0, b, :, lanes] = (grad_query * scale_ref[:, 0:1]).astype(bf16)
    for j in range(count):
        at = slice(j * size, (j + 1) * size)
        grad_ref[1, j, :, :size] = grad_keys[at, :].T.astype(bf16)
        grad_ref[2, j, :, :size] = grad_values[at, :].T.astype(bf16)
    sum_ref[...] = jnp.broadcast_to(scale_sum, sum_ref.shape)
    twice = spread_ref.shape[1] // 3
    for m in range(3):
        left = jnp.zeros((twice, head_dim), f32)
        for b in range(count):
            terms = spread_ref[b, m * twice : (m + 1) * twice]
            left += dot(terms, grad_ref[m, b], NT)
        left_ref[0, m, :, :head_dim] = left[: twice // 2] + left[twice // 2 :]


def attend_back(valid, places, qkv, query, att, lse, query_scale, terms, parts, heads, head_dim):
    count, three_own, rows = qkv.shape
    own = three_own // 3
    size = PROMPT // count
    block = lambda kind: pl.BlockSpec(
        (count, head_dim, rows), lambda h, *_: (0, kind * heads + h, 0)
    )
    pairs = PROMPT * PROMPT // 2 + PROMPT * count * (rows - size)
    return pl.pallas_call(
        attend_back_body,
        out_shape=(
            jax.ShapeDtypeStruct((3, count, own, rows), bf16),
            jax.ShapeDtypeStruct((own, LANES), f32),
            jax.ShapeDtypeStruct((heads, 3, terms.shape[1] // 6, LANES), f32),
        ),
        grid_spec=pltpu.PrefetchScalarGridSpec(
            num_scalar_prefetch=2,
            grid=(heads,),
            in_specs=[
                block(0),
                block(1),
                block(2),
                block(0),
                block(0),
                pl.BlockSpec((1, count, rows), lambda h, *_: (h, 0, 0)),
                pl.BlockSpec((head_dim, 1), lambda h, *_: (h, 0)),
                pl.BlockSpec(terms.shape, lambda h, *_: (0, 0, 0)),
            ]
            + [
                pl.BlockSpec((1, head_dim, rows), lambda h, *_: (0, h, 0))
                if part.ndim == 3
                else pl.BlockSpec((head_dim, rows), lambda h, *_: (h, 0))
                for part in parts
            ],
            out_specs=[
                pl.BlockSpec((3, count, head_dim, rows), lambda h, *_: (0, 0, h, 0)),
                pl.BlockSpec((head_dim, LANES), lambda h, *_: (h, 0)),
                pl.BlockSpec((1, 3, terms.shape[1] // 6, LANES), lambda h, *_: (h, 0, 0, 0)),
            ],
            scratch_shapes=[
                pltpu.VMEM((PROMPT, head_dim), bf16),
                pltpu.VMEM((PROMPT, head_dim), bf16),
                pltpu.VMEM((PROMPT, head_dim), f32),
                pltpu.VMEM((PROMPT, head_dim), f32),
                pltpu.VMEM((count, head_dim, rows), bf16),
            ],
        ),
        compiler_params=params(),
        cost_estimate=cost(10 * 256 * heads * pairs, qkv.size * 5),
    )(valid, places, qkv, qkv, qkv, query, att, lse, query_scale, terms, *parts)


def feed_body(place_ref, tok_ref, cot_ref, vec_ref, *refs):
    count = (place_ref.shape[0] - 1) // 3
    far = count // 2 - 1
    att_parts = refs[:count]
    w_own, w_pair, *w_far = refs[count : count + 10]
    outs = refs[count + 10 :]
    att_grad_outs, outs = outs[: far + 2], outs[far + 2 :]
    (
        result_out,
        hidden_grad_out,
        inputs_out,
        grads_out,
        sums_ref,
        w,
        att,
        hidden,
        weighted,
        inputs,
        grads,
        result,
        att_grad,
        att_sems,
        w_sems,
        out_sems,
    ) = outs
    rows, width = tok_ref.shape
    own = width // count
    quarter = own // 4
    tile = 2 * LANES
    tiles = width // tile

    def load(source, target, sem):
        one = pltpu.make_async_copy(source, target, sem)
        one.start()
        return one

    att_copies = [
        load(
            att_parts[i].at[0] if i > 1 and i % 2 == 0 else att_parts[i],
            att.at[place_ref[count + i]],
            att_sems.at[i],
        )
        for i in range(count)
    ]
    w_copies = []
    for m in range(3):
        group = []
        for flip in range(2):
            source = w_pair.at[m] if flip else w_own.at[3 + m]
            group.append(load(source, w.at[m, place_ref[count + flip]], w_sems.at[m, len(group)]))
            pieces = w_far[4 * flip : 4 * flip + 4]
            for s in range(far):
                at = place_ref[count + 2 * (s + 1) + flip]
                for i in range(4):
                    start = pl.multiple_of((place_ref[3 * count] ^ i) * quarter, quarter)
                    target = w.at[m, at, pl.ds(start, quarter), :]
                    group.append(load(pieces[i].at[s, m], target, w_sems.at[m, len(group)]))
        w_copies.append(group)
    stores = []

    def store(source, target):
        stores.append(load(source, target, out_sems.at[len(stores)]))

    def rows_of(ref, p):
        return ref.at[pl.ds(pl.multiple_of(place_ref[2 * count + p] * own, own), own), :]

    def store_grads(m):
        for p in range(count):
            store(rows_of(grads.at[m], p), grads_out.at[m, p])

    grad_f = cot_ref[...]
    grads[2] = grad_f.T
    store_grads(2)
    for one in att_copies:
        one.wait()
    attended = att[...].reshape(width, rows).T
    inputs[0] = attended
    store(inputs.at[0], inputs_out.at[0])

    def w_rows(m, j):
        return w.at[m].reshape(width, width)[pl.ds(pl.multiple_of(j * tile, tile), tile), :]

    def w_cols(m, j):
        return w.at[m].reshape(width, width)[:, pl.ds(pl.multiple_of(j * tile, tile), tile)]

    def lanes(j):
        return pl.ds(pl.multiple_of(j * tile, tile), tile)

    for one in w_copies[0]:
        one.wait()

    def first(j, square):
        part = tok_ref[:, lanes(j)].astype(f32) + dot(attended, w_rows(0, j), NT)
        hidden[:, lanes(j)] = part
        return square + jnp.sum(part * part, axis=-1, keepdims=True)

    square = lax.fori_loop(0, tiles, first, jnp.zeros((rows, 1), f32), unroll=True)
    scale = lax.rsqrt(square / width + EPS)
    normed = (hidden[...] * scale * vec_ref[1:2, :]).astype(bf16)
    inputs[1] = normed
    store(inputs.at[1], inputs_out.at[1])
    for m in (1, 2):
        for one in w_copies[m]:
            one.wait()

    def second(j, carry):
        upper = dot(normed, w_rows(1, j), NT) + vec_ref[2:3, lanes(j)]
        gate = 1.0 / (1.0 + jnp.exp(-upper))
        inputs[2, :, lanes(j)] = (upper * gate).astype(bf16)
        grad_act = dot(grad_f, w_cols(2, j), NN)
        grad_up = (grad_act * gate * (1.0 + upper * (1.0 - gate))).astype(bf16)
        result[:, lanes(j)] = grad_up
        sums_ref[1:2, lanes(j)] = jnp.sum(grad_up.astype(f32), axis=0, keepdims=True)
        sums_ref[2:3, lanes(j)] = jnp.sum(
            cot_ref[:, lanes(j)].astype(f32), axis=0, keepdims=True
        )
        return carry

    lax.fori_loop(0, tiles, second, 0, unroll=True)
    store(inputs.at[2], inputs_out.at[2])
    grad_up = result[...]
    grads[1] = grad_up.T
    store_grads(1)
    activ = inputs[2]

    def third(j, inner):
        part = hidden[:, lanes(j)]
        out = dot(activ, w_rows(2, j), NT) + vec_ref[3:4, lanes(j)]
        result[:, lanes(j)] = (part + out).astype(bf16)
        grad_normed = dot(grad_up, w_cols(1, j), NN)
        sums_ref[0:1, lanes(j)] = jnp.sum(grad_normed * part * scale, axis=0, keepdims=True)
        turn = grad_normed * vec_ref[1:2, lanes(j)]
        weighted[:, lanes(j)] = turn
        return inner + jnp.sum(part * turn, axis=-1, keepdims=True)

    inner = lax.fori_loop(0, tiles, third, jnp.zeros((rows, 1), f32), unroll=True) / width
    store(result, result_out)
    back = cot_ref[...].astype(f32) + (
        scale * weighted[...] - hidden[...] * (scale * scale * scale) * inner
    )
    weighted[...] = back
    store(weighted, hidden_grad_out)
    branch = back.astype(bf16)

    def fourth(j, carry):
        att_grad[lanes(j), :] = dot(branch, w_cols(0, j), NN).astype(bf16).T
        return carry

    lax.fori_loop(0, tiles, fourth, 0, unroll=True)
    for p in range(count):
        target = att_grad_outs[p] if p < 2 else att_grad_outs[p // 2 + 1].at[p % 2]
        store(rows_of(att_grad, (p % 2) * (far + 1) + p // 2), target)
    grads[0] = branch.T
    store_grads(0)
    for one in stores:
        one.wait()


def feed(places, tokens, cotangent, vec, att_parts, w_parts):
    count = len(att_parts)
    rows, width = tokens.shape
    own = width // count
    whole = lambda *shape: pl.BlockSpec(shape, lambda i, at: (0,) * len(shape))
    return pl.pallas_call(
        feed_body,
        out_shape=(
            *[jax.ShapeDtypeStruct((own, rows), bf16)] * 2,
            *[jax.ShapeDtypeStruct((2, own, rows), bf16)] * (count // 2 - 1),
            jax.ShapeDtypeStruct((rows, width), bf16),
            jax.ShapeDtypeStruct((rows, width), f32),
            jax.ShapeDtypeStruct((3, rows, width), bf16),
            jax.ShapeDtypeStruct((3, count, own, rows), bf16),
            jax.ShapeDtypeStruct((8, width), f32),
        ),
        grid_spec=pltpu.PrefetchScalarGridSpec(
            num_scalar_prefetch=1,
            grid=(1,),
            in_specs=[whole(rows, width), whole(rows, width), whole(*vec.shape)]
            + [ANY] * (count + len(w_parts)),
            out_specs=[ANY] * (5 + count // 2) + [whole(8, width)],
            scratch_shapes=[
                pltpu.VMEM((3, count, own, width), bf16),
                pltpu.VMEM((count, own, rows), bf16),
                pltpu.VMEM((rows, width), f32),
                pltpu.VMEM((rows, width), f32),
                pltpu.VMEM((3, rows, width), bf16),
                pltpu.VMEM((3, width, rows), bf16),
                pltpu.VMEM((rows, width), bf16),
                pltpu.VMEM((width, rows), bf16),
                pltpu.SemaphoreType.DMA((count,)),
                pltpu.SemaphoreType.DMA((3, 2 + 8 * (count // 2 - 1))),
                pltpu.SemaphoreType.DMA((5 + 4 * count,)),
            ],
        ),
        compiler_params=params(),
        cost_estimate=cost(12 * rows * width * width, 3 * width * width * 2 + rows * width * 24),
    )(places, tokens, cotangent, vec, *att_parts, *w_parts)


def split(x):
    high = x.astype(bf16)
    return jnp.concatenate([high, (x - high.astype(f32)).astype(bf16)], axis=-2)


def fold(x, rank):
    return x[..., :rank, :] + x[..., rank:, :]


def outer_body(grad_ref, input_ref, right_ref, *refs):
    *outs, left_mine_ref, left_away_ref = refs
    count, own, rows = grad_ref.shape[1:]
    chips = count // 2
    twice = right_ref.shape[1]
    grads = grad_ref[0]
    out = dot(grads.reshape(count * own, rows), input_ref[0], NN).astype(bf16)
    for b in range(count):
        outs[b][0] = out[b * own : (b + 1) * own]
    spread = dot(right_ref[...].reshape(count * twice, -1), input_ref[0], NT)
    for b in range(count):
        terms = split(fold(spread[b * twice : (b + 1) * twice], twice // 2))
        left = fold(dot(terms, grads[b], NT), twice // 2)
        if b < chips:
            left_mine_ref[b, 0] = left
        else:
            left_away_ref[b - chips, 0] = left


def outer(grads, inputs, rights):
    mats, count, own, rows = grads.shape
    width = count * own
    twice = rights.shape[1] // mats
    chips = count // 2
    left = jax.ShapeDtypeStruct((chips, mats, twice // 2, own), f32)
    part = jax.ShapeDtypeStruct((mats, own, width), bf16)
    part_spec = pl.BlockSpec((1, own, width), lambda m: (m, 0, 0))
    left_spec = pl.BlockSpec((chips, 1, twice // 2, own), lambda m: (0, m, 0, 0))
    return pl.pallas_call(
        outer_body,
        out_shape=(*[part] * count, left, left),
        grid=(mats,),
        in_specs=[
            pl.BlockSpec((1, count, own, rows), lambda m: (m, 0, 0, 0)),
            pl.BlockSpec((1, rows, width), lambda m: (m, 0, 0)),
            pl.BlockSpec((count, twice, width), lambda m: (0, m, 0)),
        ],
        out_specs=[part_spec] * count + [left_spec] * 2,
        compiler_params=params(),
        cost_estimate=cost(2 * mats * width * width * rows, mats * width * (width + rows) * 4),
    )(grads, inputs, rights)


def spread_body(normed_ref, right_ref, out_ref):
    mats_twice = right_ref.shape[0]
    twice = mats_twice // 3
    out = dot(right_ref[...], normed_ref[0], NT)
    for m in range(3):
        at = slice(m * twice, (m + 1) * twice)
        out_ref[0, at] = split(fold(out[at], twice // 2))


def spread(normed, rights):
    count, rows, width = normed.shape
    size = rights.shape[0]
    return pl.pallas_call(
        spread_body,
        out_shape=jax.ShapeDtypeStruct((count, size, rows), bf16),
        grid=(count,),
        in_specs=[
            pl.BlockSpec((1, rows, width), lambda b: (b, 0, 0)),
            pl.BlockSpec((size, width), lambda b: (0, 0)),
        ],
        out_specs=pl.BlockSpec((1, size, rows), lambda b: (b, 0, 0)),
        compiler_params=params(),
        cost_estimate=cost(2 * count * rows * width * size, normed.size * 2),
    )(normed, rights)


def error_left_body(error_ref, right_ref, out_ref):
    rank = right_ref.shape[1]
    error = error_ref[0]
    high = error.astype(bf16)
    low = (error - high.astype(f32)).astype(bf16)
    rights = split(right_ref[0])
    out = dot(high, rights, NT) + dot(low, rights, NT)
    out_ref[0] = fold(out.T, rank)


def error_left(error, right):
    mats, own, width = error.shape
    rank = right.shape[1]
    return pl.pallas_call(
        error_left_body,
        out_shape=jax.ShapeDtypeStruct((mats, rank, own), f32),
        grid=(mats,),
        in_specs=[
            pl.BlockSpec((1, own, width), lambda m: (m, 0, 0)),
            pl.BlockSpec((1, rank, width), lambda m: (m, 0, 0)),
        ],
        out_specs=pl.BlockSpec((1, rank, own), lambda m: (m, 0, 0)),
        compiler_params=params(),
        cost_estimate=cost(4 * error.size * rank, error.size * 4),
    )(error, right)


def input_back_body(order_ref, grad_ref, w_ref, *refs):
    count = len(refs) - 2
    tok_refs = refs[:count]
    out_ref, sum_ref = refs[count:]
    step = pl.program_id(0)
    own, rows = grad_ref.shape[2:]
    grads = grad_ref[...].reshape(3 * own, rows)
    part = dot(grads, w_ref[...].reshape(3 * own, -1), TN)
    out_ref[0] = part.astype(bf16)
    tok = tok_refs[0][...]
    for i in range(1, count):
        tok = jnp.where(step == i, tok_refs[i][...], tok)
    tok = tok.astype(f32)
    total = jnp.sum(part * (tok * rms_scale(tok)), axis=0, keepdims=True)

    @pl.when(step == 0)
    def _():
        sum_ref[...] = jnp.zeros_like(sum_ref)

    sum_ref[...] += jnp.broadcast_to(total, sum_ref.shape)


def input_back(maps, flip, grads, w_mats, toks):
    _, total, own, rows = grads.shape
    count = total // 2
    first = 2 * total + flip * count
    width = w_mats.shape[-1]
    return pl.pallas_call(
        input_back_body,
        out_shape=(
            jax.ShapeDtypeStruct((count, rows, width), bf16),
            jax.ShapeDtypeStruct((8, width), f32),
        ),
        grid_spec=pltpu.PrefetchScalarGridSpec(
            num_scalar_prefetch=1,
            grid=(count,),
            in_specs=[
                pl.BlockSpec((3, 1, own, rows), lambda s, at: (0, at[first + s], 0, 0)),
                pl.BlockSpec((3, own, width), lambda s, at: (0, 0, 0)),
            ]
            + [pl.BlockSpec((rows, width), lambda s, at: (0, 0))] * count,
            out_specs=[
                pl.BlockSpec((1, rows, width), lambda s, at: (s, 0, 0)),
                pl.BlockSpec((8, width), lambda s, at: (0, 0)),
            ],
        ),
        compiler_params=params(),
        cost_estimate=cost(2 * grads.size * width, grads.size * 2 + count * rows * width * 4),
    )(maps, grads, w_mats, *toks)


def right_body(ortho_ref, *refs):
    *terms, out = refs
    merged = sum(term[0].astype(f32) for term in terms)
    rank = ortho_ref.shape[1]
    out[0] = fold(dot(split(ortho_ref[0]), merged.astype(bf16), NN), rank).astype(bf16)


def tile_specs(rows, tile, first):
    return (
        pl.BlockSpec((1, rows, tile), lambda m, j: (first + m, 0, j)),
        pl.BlockSpec((1, rows, tile), lambda m, j: (m, 0, j)),
    )


def right_factors(ortho, error, first, terms):
    mats, own, width = terms[0].shape
    rank = ortho.shape[1]
    tile = width
    error_spec, term_spec = tile_specs(own, tile, first)
    return pl.pallas_call(
        right_body,
        out_shape=jax.ShapeDtypeStruct((mats, rank, width), bf16),
        grid=(mats, width // tile),
        in_specs=[pl.BlockSpec((1, rank, own), lambda m, j: (first + m, 0, 0)), error_spec]
        + [term_spec] * len(terms),
        out_specs=tile_specs(rank, tile, first)[1],
        compiler_params=params(2),
        cost_estimate=cost(4 * mats * own * width * rank, mats * own * width * 6),
    )(ortho, error, *terms)


def triple(x, pattern):
    high = x.astype(bf16)
    low = (x - high.astype(f32)).astype(bf16)
    return jnp.concatenate([low if p else high for p in pattern], axis=0)


def finish_body(rate, count, ortho_ref, right_ref, slice_ref, mom_ref, *refs):
    terms = refs[:count]
    err_ref, fresh_ref, grad_ref, new_ref, upd_ref = refs[-5:]
    ortho = triple(ortho_ref[0], (0, 0, 1))
    fresh_ref[0] = right_ref[0]
    approx = dot(ortho, triple(right_ref[0], (0, 1, 0)), TN)
    err_ref[0] = sum(term[0].astype(f32) for term in terms) - approx

    @pl.when(pl.program_id(1) == 0)
    def _():
        grad = dot(triple(slice_ref[0], (0, 1, 0)), ortho, TN)
        grad_ref[0] = grad
        new = MU * mom_ref[0] + grad
        new_ref[0] = new
        upd_ref[0] = -rate * new


def finish(rate, ortho, right, right_slice, momentum, error, first, terms, held):
    half, own, width = terms[0].shape
    mats, rank = ortho.shape[:2]
    cut = momentum.shape[1]
    tile = width
    error_spec, term_spec = tile_specs(own, tile, first)
    fresh_spec, right_spec = tile_specs(rank, tile, first)
    per = lambda *shape: pl.BlockSpec((1,) + shape, lambda m, j: (m, 0, 0))
    at = lambda *shape: pl.BlockSpec((1,) + shape, lambda m, j: (first + m, 0, 0))
    shape = jax.ShapeDtypeStruct(momentum.shape, f32)
    held = () if held is None else tuple(held)
    return pl.pallas_call(
        functools.partial(finish_body, rate, 1 + len(terms)),
        out_shape=(
            jax.ShapeDtypeStruct((mats, own, width), f32),
            jax.ShapeDtypeStruct((mats, rank, width), f32),
            shape,
            shape,
            shape,
        ),
        grid=(half, width // tile),
        in_specs=[at(rank, own), right_spec, per(rank, cut), at(cut, own), error_spec]
        + [term_spec] * len(terms)
        + [ANY] * len(held),
        out_specs=[error_spec, fresh_spec] + [at(cut, own)] * 3,
        input_output_aliases={5 + len(terms) + i: i for i in range(len(held))},
        compiler_params=params(2),
        cost_estimate=cost(half * own * width * 48, half * own * width * 10),
    )(ortho, right, right_slice, momentum, error, *terms, *held)


def close_rows_body(tok_ref, gain_ref, hidden_ref, mine_ref, paired_ref, *refs):
    *far, out = refs
    grad = mine_ref[0].astype(f32) + paired_ref[0].astype(f32)
    for term in far:
        grad += term[...].astype(f32)
    tok = tok_ref[...].astype(f32)
    out[...] = hidden_ref[...] + norm_back(tok, rms_scale(tok), gain_ref[...], grad)


def close_rows(tokens, gain, grad_hidden, mine, paired, far):
    rows, width = tokens.shape
    row = pl.BlockSpec((LANES, width), lambda i: (i, 0))
    first = pl.BlockSpec((1, LANES, width), lambda i: (0, i, 0))
    return pl.pallas_call(
        close_rows_body,
        out_shape=jax.ShapeDtypeStruct((rows, width), f32),
        grid=(rows // LANES,),
        in_specs=[row, pl.BlockSpec((1, width), lambda i: (0, 0)), row, first, first]
        + [row] * len(far),
        out_specs=row,
        compiler_params=params(),
        cost_estimate=cost(20 * rows * width, 18 * rows * width),
    )(tokens, gain, grad_hidden, mine, paired, *far)


def ortho_body(left_ref, out_ref):
    rank = left_ref.shape[0]
    columns = [left_ref[c] for c in range(rank)]
    for e in range(rank):
        done = columns[e]
        done = done * lax.rsqrt(jnp.sum(done * done, axis=-1, keepdims=True) + EPS)
        out_ref[:, e, :] = done
        for c in range(e + 1, rank):
            columns[c] = columns[c] - jnp.sum(done * columns[c], axis=-1, keepdims=True) * done


def orthonormal(left):
    rank, mats, own = left.shape
    return pl.pallas_call(
        ortho_body, out_shape=jax.ShapeDtypeStruct((mats, rank, own), f32)
    )(left)


def on_device(
    tokens,
    cotangent,
    weights,
    vectors,
    error,
    previous_right_factors,
    momentum,
    vec_momentum,
    prompt_len,
):
    zero_index = lax.axis_index("zero")
    rep_index = lax.axis_index("rep")
    n = lax.axis_size("zero")
    chips = n // 2
    rep_count = lax.axis_size("rep")
    rows, width = tokens.shape
    head_dim = width // HEADS
    heads = HEADS // n
    own = weights.shape[0]
    group_rows = n * rows
    quarter = rep_index & 3
    maps = tables(zero_index >> 1, zero_index & 1, chips, quarter)
    w_mats = weights.transpose(1, 0, 2)
    old_right = previous_right_factors.transpose(0, 2, 1)
    rank = old_right.shape[1]
    error_mats = error.transpose(1, 0, 2)

    column = zero_index * own
    spaced = lax.dynamic_update_slice(jnp.zeros((5, width), bf16), vectors, (0, column))
    spaced = sum((to_chip(spaced, n, s) for s in range(1, chips)), spaced)
    vec_float = (spaced + to_pair(spaced, n)).astype(f32)
    tok_parts = gather_zero(tokens, n)
    pairs_right = split(old_right)
    right_parts = gather_zero(pairs_right[3:6].reshape(6 * rank, width), n)
    flipped = [2 * ((chips - s) % chips) + f for f in range(2) for s in range(chips)]
    far_rights = jnp.stack([right_parts[i] for i in flipped])
    error_part = error_left(error_mats, old_right)
    far_parts = gather_weights(w_mats, n, quarter, rep_count)

    scale_raw = vectors[4].astype(f32)
    scale_const = LOG2E / math.sqrt(head_dim)
    query_scale = (scale_const * jax.nn.softplus(scale_raw)).reshape(own, 1)
    held = None
    for s in range(chips):
        held = project(
            maps,
            s,
            tok_parts[2 * s],
            tok_parts[2 * s + 1],
            vec_float[0:1],
            w_mats,
            query_scale,
            n,
            held,
        )
    normed_all, qkv, query = held
    *att_blocks, att_all, lse = attend(prompt_len, maps, qkv, heads, head_dim)
    att_parts = exchange_zero(att_blocks[:2], att_blocks[2:], n)
    terms = spread(normed_all, pairs_right[0:3].reshape(6 * rank, width))
    *att_grads, result, grad_hidden, far_inputs, far_grads, sums = feed(
        maps, tokens, cotangent, vec_float, att_parts, far_parts
    )
    grad_parts = exchange_zero(att_grads[:2], att_grads[2:], n)
    *blocks, left_mine, left_away = outer(far_grads, far_inputs, far_rights)
    far_sums = []
    for s in range(1, chips):
        paired = to_pair(blocks[chips + s], n)
        far_sums.append((blocks[s].astype(f32) + paired.astype(f32)).astype(bf16))
    left_far = sum(scatter_sum_zero(left_mine, left_away, n))
    grad_parts, far_sums = lax.optimization_barrier((grad_parts, far_sums))
    far_terms = [to_chip(far_sums[s - 1], n, s) for s in range(1, chips)]
    grads, scale_sums, left_heads = attend_back(
        prompt_len,
        maps,
        qkv,
        query,
        att_all,
        lse,
        query_scale,
        terms,
        grad_parts,
        heads,
        head_dim,
    )
    left_near = left_heads[..., :head_dim].transpose(1, 2, 0, 3).reshape(3, rank, own)
    left = jnp.concatenate([left_near, left_far], axis=0) + error_part
    left = sum_rep(left.transpose(1, 0, 2), rep_count) / rep_count
    ortho = orthonormal(left)

    toks = [tok_parts[i] for i in flipped]
    n1_away, gain_away = input_back(maps, 1, grads, w_mats, toks[chips:])
    n1_mine, gain_mine = input_back(maps, 0, grads, w_mats, toks[:chips])
    near = jnp.einsum("mbot,bti->moi", grads, normed_all, preferred_element_type=f32).astype(bf16)
    n1_paired = to_pair(n1_away, n)
    n1_far = []
    for s in range(1, chips):
        sent = (n1_mine[s].astype(f32) + n1_paired[s].astype(f32)).astype(bf16)
        n1_far.append(to_chip(sent, n, s))
    grad_tokens = close_rows(tokens, vec_float[0:1], grad_hidden, n1_mine, n1_paired, n1_far)

    near_terms = [near]
    far_terms = [blocks[0], to_pair(blocks[chips], n), *far_terms]
    rep_width = width // rep_count
    cut_at = rep_index * rep_width
    step_rate = 0.03 / math.sqrt(group_rows)
    momentum_mats = momentum.transpose(1, 2, 0)

    def close(right, cut_at, first, parts, held):
        own_right = lax.dynamic_slice_in_dim(right, cut_at, rep_width, 1)
        right, own_right = (x[: 3 * rank].reshape(3, rank, -1) for x in (right, own_right))
        return finish(
            step_rate, ortho, right, own_right, momentum_mats, error_mats, first, parts, held
        )

    right = right_factors(ortho, error_mats, 0, near_terms).reshape(3 * rank, width)
    right = sum_rep(right, rep_count, bf16) / rep_count
    held = close(right, cut_at, 0, near_terms, None)

    vec_sums = jnp.concatenate([gain_away[0:1] + gain_mine[0:1], sums[0:3]], axis=0)
    vec_sums = lax.dynamic_slice_in_dim(sum_zero(vec_sums, n), column, own, 1)
    grad_scale_raw = scale_sums[:, 0] * scale_const * jax.nn.sigmoid(scale_raw)
    vec_sums = jnp.concatenate([vec_sums, grad_scale_raw[None]], axis=0)
    vec_rows = -(-vec_sums.size // width)
    vec_flat = jnp.pad(vec_sums.reshape(-1), (0, vec_rows * width - vec_sums.size))
    vec_flat = vec_flat.reshape(vec_rows, width).astype(bf16)
    right = right_factors(ortho, error_mats, 3, far_terms)
    packed = jnp.concatenate([right.reshape(3 * rank, width), vec_flat], axis=0)
    packed = sum_rep(packed, rep_count, bf16) / rep_count
    held = close(packed, lax.optimization_barrier(cut_at), 3, far_terms, held)
    new_error, fresh, *moved = held
    new_error = new_error.transpose(1, 0, 2)
    fresh_right_factors = fresh.transpose(0, 2, 1)
    grad_weights, new_momentum, update_weights = (x.transpose(2, 0, 1) for x in moved)
    grad_vectors = packed[3 * rank :].reshape(-1)[: vec_sums.size].reshape(vec_sums.shape)
    new_vec_momentum = MU * vec_momentum + grad_vectors
    update_vectors = -step_rate * new_vec_momentum
    return (
        result,
        grad_tokens,
        grad_weights,
        grad_vectors,
        new_error,
        fresh_right_factors,
        new_momentum,
        new_vec_momentum,
        update_weights,
        update_vectors,
    )


def solution(mesh):
    in_specs = (
        P(("rep", "zero"), None),
        P(("rep", "zero"), None),
        P("zero", None, None),
        P(None, "zero"),
        P(("rep", "zero"), None, None),
        P(None, None, "zero"),
        P("zero", None, "rep"),
        P(None, "zero"),
        P("rep"),
    )
    out_specs = (
        P(("rep", "zero"), None),
        P(("rep", "zero"), None),
        P("zero", None, "rep"),
        P(None, "zero"),
        P(("rep", "zero"), None, None),
        P(None, None, "zero"),
        P("zero", None, "rep"),
        P(None, "zero"),
        P("zero", None, "rep"),
        P(None, "zero"),
    )

    return jax.shard_map(
        on_device, mesh=mesh, in_specs=in_specs, out_specs=out_specs, check_vma=False
    )
```
